128 devices in a mesh: seq: 4 (over y), exp: 32 (over z, x, core).
Axes of the slice: x: 4, y: 4, z: 4, core: 2. Of those that a mesh axis runs over, the one named last changes fastest.
Arguments:
- queries: bfloat16 [32, 512, 4096], P('exp', 'seq'), may hold values from -36 to 36
- rotated_keys: bfloat16 [32, 512, 512], P('exp', 'seq'), may hold values from -4 to 4
- projected_values: bfloat16 [32, 512, 512], P('exp', 'seq'), may hold values from -4 to 4
- doc_ids: int32 [32, 512], P('exp'), may hold values from 0 to 3, never falling along the last dimension, each value on 1 to 256 neighbouring positions
- residual: bfloat16 [32, 512, 4096], P('exp', 'seq'), may hold values from -14 to 14
- out_weight: bfloat16 [4096, 4096], P('seq', 'exp'), may hold values from -0.09375 to 0.09375
- norm_gain: float32 [4096], replicated, may hold values from 0.1 to 1.9
- routes: int32 [32, 512, 8], P('exp', 'seq'), may hold values from 0 to 127, as said below
- gate_vals: float32 [32, 512, 8], P('exp', 'seq'), may hold values from 0.05 to 0.35
- cotangent: bfloat16 [32, 512, 4096], P('exp', 'seq'), may hold values from -0.119628906 to 0.119628906
- expert_in: bfloat16 [128, 4096, 1536], P(('seq', 'exp')), may hold values from -0.09375 to 0.09375
- expert_down: bfloat16 [128, 768, 4096], P(('seq', 'exp')), may hold values from -0.21875 to 0.21875
Outputs:
- layer_out: bfloat16 [32, 512, 4096], P('exp', 'seq')
- gate_grad: float32 [32, 512, 8], P('exp', 'seq')
The draws below stay inside these ranges and needn't reach their ends.
Inputs may be any that keep to these rules, and one draw needn't show every extreme that they name: `routes`: each token names 8 different experts; the tokens of one device name no expert more than 10 times, and one expert, the same for all devices, exactly 10 times on every device. `doc_ids`: document numbers never fall along a pack; a document holds at most 256 positions.
All inputs are finite; a program needn't handle non-finite values.
Results may differ from the reference program's by a relative error of at most 0.0067.
Values may be sent and summed in bfloat16 or wider, within the bound.
No kernel may reach another device: no remote copies, remote signals or barrier semaphores. Data moves between devices by JAX's collectives and lax.ppermute only.
A program may use at most 192 MiB of HBM per device.

```python
import math
import jax
import jax.numpy as jnp
import numpy as np
from jax import lax

D = 4096
QUERY_HEADS = 32
KEY_VALUE_HEADS = 4
HEAD_SIZE = 128
HID = 768
TOPK = 8
TOK_DEV = 128
EXPERTS = 128
PACK_LENGTH = 512
PACK_COUNT = 32
CAP = 10


def draw_queries(key, part):
    value_entries = jax.random.truncated_normal(jax.random.fold_in(key, 1), -4.0, 4.0, (PACK_COUNT, PACK_LENGTH, QUERY_HEADS * HEAD_SIZE), jnp.float32)
    return value_entries.astype(jnp.bfloat16)


def draw_rotated_keys(key, part):
    value_entries = jax.random.truncated_normal(jax.random.fold_in(key, 2), -4.0, 4.0, (PACK_COUNT, PACK_LENGTH, KEY_VALUE_HEADS * HEAD_SIZE), jnp.float32)
    return value_entries.astype(jnp.bfloat16)


def draw_residual(key, part):
    value_entries = jax.random.truncated_normal(jax.random.fold_in(key, 3), -4.0, 4.0, (PACK_COUNT, PACK_LENGTH, D), jnp.float32)
    return value_entries.astype(jnp.bfloat16)


def draw_routes(key, part):
    block_total = PACK_COUNT * (PACK_LENGTH // TOK_DEV)
    pair_count = TOK_DEV * TOPK
    hot_expert = jax.random.randint(jax.random.fold_in(key, 7), (), 0, EXPERTS)
    remaining = pair_count - CAP
    base_count = remaining // (EXPERTS - 1)
    extra_count = remaining - base_count * (EXPERTS - 1)
    half_count = (EXPERTS - 1) // 2

    def one_block(block_key):
        order_rank = jax.random.permutation(jax.random.fold_in(block_key, 1), EXPERTS - 1)
        counts = base_count + (order_rank < extra_count).astype(jnp.int32)
        givers = counts[:half_count]
        takers = counts[half_count:2 * half_count]
        room_left = jnp.minimum(givers, CAP - takers)
        moved = jax.random.randint(jax.random.fold_in(block_key, 2), (half_count,), 0, room_left + 1)
        counts = counts.at[:half_count].add(-moved).at[half_count:2 * half_count].add(moved)
        counts = jnp.concatenate([jnp.full((1,), CAP, jnp.int32), counts.astype(jnp.int32)])
        ends_at = jnp.cumsum(counts)
        virtual = jnp.searchsorted(ends_at, jnp.arange(pair_count, dtype=jnp.int32), side='right').astype(jnp.int32)
        relabel = jax.random.permutation(jax.random.fold_in(block_key, 3), EXPERTS).astype(jnp.int32)
        hot_place = jnp.argmax((relabel == hot_expert).astype(jnp.int32))
        relabel = relabel.at[hot_place].set(relabel[0]).at[0].set(hot_expert)
        labels = relabel[virtual]
        routed = labels.reshape(TOPK, TOK_DEV).T
        token_order = jax.random.permutation(jax.random.fold_in(block_key, 4), TOK_DEV)
        return routed[token_order]
    block_keys = jax.random.split(jax.random.fold_in(key, 8), block_total)
    routed_all = jax.vmap(one_block)(block_keys)
    return routed_all.reshape(PACK_COUNT, PACK_LENGTH, TOPK).astype(jnp.int32)


def shard_levels(key, extent, cuts, low, largest):
    loudness, own = 1.0, jax.random.fold_in(key, 6)
    for position, shards_of in cuts:
        draws = jnp.exp(jax.random.uniform(jax.random.fold_in(own, position), (shards_of,), jnp.float32, low / len(cuts), largest / len(cuts)))
        loudness = loudness * jnp.repeat(draws, extent[position] // shards_of).reshape([-1 if axis == position else 1 for axis in range(len(extent))])
    return loudness


def split_up(number_of, total, bound, skew):
    portions = [(1 << 20) // math.isqrt(standing ** skew) + 1 for standing in range(2, number_of + 1)]
    spare, given = total - bound - (number_of - 1), [1] * (number_of - 1)
    while spare > 0:
        free = [i for i in range(number_of - 1) if given[i] < bound]
        mass, budget = sum([portions[i] for i in free]), spare
        for i in free:
            more = min(bound - given[i], max(1, budget * portions[i] // mass), spare)
            given[i] = given[i] + more
            spare = spare - more
    return np.array([bound] + given)


def ragged_sizes(stream_key, count, total, reach, slope):
    if count == 2:
        one = jax.random.randint(stream_key, (), max(1, total - reach), min(reach, total - 1) + 1)
        return jnp.stack([one, total - one])
    sizes = jnp.asarray(split_up(count, total, reach, slope), jnp.int32)
    pairs = (count - 1) // 2
    donor, sink = sizes[1:1 + 2 * pairs:2], sizes[2:2 + 2 * pairs:2]
    room = jnp.minimum(donor - 1, reach - sink)
    moved = jax.random.randint(jax.random.fold_in(stream_key, 1), (pairs,), 0, 1 << 20) % (room + 1)
    sizes = sizes.at[1:1 + 2 * pairs:2].set(donor - moved).at[2:2 + 2 * pairs:2].set(sink + moved)
    return sizes[jax.random.permutation(jax.random.fold_in(stream_key, 2), count)]


def noise(own_key, extent, deviation, most, pieces=(), kind=jnp.bfloat16):
    loudness = shard_levels(own_key, extent, pieces, -0.22, 0.18) if pieces else 1.0
    values = jax.random.normal(own_key, extent, jnp.float32) * deviation * loudness
    return jnp.minimum(jnp.maximum(values, -most), most).astype(kind)


def setup_inputs(seed: int = 0) -> dict:
    key_list = jax.random.split(jax.random.key(seed), 13)
    queries = draw_queries(jax.random.fold_in(key_list[12], 71), 0)
    rotated_keys = draw_rotated_keys(jax.random.fold_in(key_list[12], 71), 0)
    projected_values = noise(key_list[2], (PACK_COUNT, PACK_LENGTH, KEY_VALUE_HEADS * HEAD_SIZE), 1.0, 4.0, ((0, 32), (1, 4)))
    doc_ids = jax.vmap(lambda own: jnp.searchsorted(jnp.cumsum(ragged_sizes(own, max(4, PACK_LENGTH // 128), PACK_LENGTH, PACK_LENGTH // 2, 2)), jnp.arange(PACK_LENGTH), side="right"))(jax.random.split(key_list[3], PACK_COUNT)).reshape((PACK_COUNT, PACK_LENGTH)).astype(jnp.int32)
    residual = draw_residual(jax.random.fold_in(key_list[12], 71), 0)
    out_weight = noise(key_list[5], (QUERY_HEADS * HEAD_SIZE, D), (QUERY_HEADS * HEAD_SIZE) ** -0.5, 0.09375, ((0, 4), (1, 32)))
    norm_gain = jnp.clip(1.0 + 0.18 * jax.random.normal(key_list[6], (D,), jnp.float32), 0.1, 1.9)
    routes = draw_routes(jax.random.fold_in(key_list[12], 71), 0)
    gate_vals = jnp.clip(0.05 + 0.29999999 * jax.random.uniform(key_list[8], (PACK_COUNT, PACK_LENGTH, TOPK), jnp.float32) ** shard_levels(key_list[8], (PACK_COUNT, PACK_LENGTH, TOPK), ((0, 32), (1, 4)), -0.2, 0.2), 0.05, 0.35)
    cotangent = noise(key_list[9], (PACK_COUNT, PACK_LENGTH, D), 0.02, 0.119628906, ((0, 32), (1, 4)))
    expert_in = noise(key_list[10], (EXPERTS, D, 2 * HID), D ** -0.5, 0.09375, ((0, 128),))
    expert_down = noise(key_list[11], (EXPERTS, HID, D), HID ** -0.5, 0.21875, ((0, 128),))
    return dict(queries=queries, rotated_keys=rotated_keys, projected_values=projected_values, doc_ids=doc_ids, residual=residual, out_weight=out_weight, norm_gain=norm_gain, routes=routes, gate_vals=gate_vals, cotangent=cotangent, expert_in=expert_in, expert_down=expert_down)


def attend(queries, rotated_keys, projected_values, doc_ids):
    grouping_factor = QUERY_HEADS // KEY_VALUE_HEADS
    query_head_rows = queries.reshape(PACK_LENGTH, KEY_VALUE_HEADS, grouping_factor, HEAD_SIZE)
    key_head_rows = rotated_keys.reshape(PACK_LENGTH, KEY_VALUE_HEADS, HEAD_SIZE)
    value_head_rows = projected_values.reshape(PACK_LENGTH, KEY_VALUE_HEADS, HEAD_SIZE)
    positions = jnp.arange(PACK_LENGTH)
    allowed = (positions[None, :] <= positions[:, None]) & (doc_ids[None, :] == doc_ids[:, None])
    score_scale = 1.0 / math.sqrt(HEAD_SIZE)

    def head_results(head_index):
        query_group = lax.dynamic_index_in_dim(query_head_rows, head_index, 1, keepdims=False).astype(jnp.float32)
        key_group = lax.dynamic_index_in_dim(key_head_rows, head_index, 1, keepdims=False).astype(jnp.float32)
        value_group = lax.dynamic_index_in_dim(value_head_rows, head_index, 1, keepdims=False).astype(jnp.float32)
        scores = jnp.einsum('igd,jd->gij', query_group, key_group) * score_scale
        scores = jnp.where(allowed[None], scores, -jnp.inf)
        row_max = lax.optimization_barrier(jnp.max(scores, axis=-1, keepdims=True))
        raised = jnp.exp(scores - row_max)
        weights_bf = (raised / lax.optimization_barrier(jnp.sum(raised, axis=-1, keepdims=True))).astype(jnp.bfloat16)
        weights_back = lax.optimization_barrier(weights_bf).astype(jnp.float32)
        head_out = jnp.einsum('gij,jd->igd', weights_back, value_group)
        return head_out.astype(jnp.bfloat16)
    output_rows = lax.map(head_results, jnp.arange(KEY_VALUE_HEADS))
    return jnp.transpose(output_rows, (1, 0, 2, 3)).reshape(PACK_LENGTH, QUERY_HEADS * HEAD_SIZE)

def reference(queries, rotated_keys, projected_values, doc_ids, residual, out_weight, norm_gain, routes, gate_vals, cotangent, expert_in, expert_down):
    attended = lax.map(lambda items: attend(items[0], items[1], items[2], items[3]), (queries, rotated_keys, projected_values, doc_ids))
    projected = jnp.dot(attended.reshape(PACK_COUNT * PACK_LENGTH, QUERY_HEADS * HEAD_SIZE), out_weight, preferred_element_type=jnp.float32)
    hidden_state = residual.reshape(PACK_COUNT * PACK_LENGTH, D).astype(jnp.float32) + projected
    root_mean = jnp.sqrt(lax.optimization_barrier(jnp.mean(hidden_state * hidden_state, axis=-1, keepdims=True)) + 1e-06)
    normed = (hidden_state / root_mean * norm_gain).astype(jnp.bfloat16)
    flat_routes = routes.reshape(-1)
    flat_gates = gate_vals.reshape(-1)
    flat_cotangent = cotangent.reshape(PACK_COUNT * PACK_LENGTH, D)
    slot_limit = CAP * EXPERTS

    def per_expert(carry, expert_id):
        accumulated, gradient = carry
        matches = flat_routes == expert_id
        pair_ids = jnp.nonzero(matches, size=slot_limit, fill_value=0)[0].astype(jnp.int32)
        is_live = jnp.arange(slot_limit) < jnp.sum(matches.astype(jnp.int32))
        token_ids = pair_ids // TOPK
        taken = normed[token_ids]
        gate_up = jnp.dot(taken, expert_in[expert_id], preferred_element_type=jnp.float32)
        activated = (jax.nn.silu(gate_up[:, :HID]) * gate_up[:, HID:]).astype(jnp.bfloat16)
        expert_out = jnp.dot(activated, expert_down[expert_id], preferred_element_type=jnp.float32).astype(jnp.bfloat16)
        out_back = lax.optimization_barrier(expert_out).astype(jnp.float32)
        weighted = jnp.where(is_live, flat_gates[pair_ids], jnp.float32(0.0))
        accumulated = accumulated.at[token_ids].add(weighted[:, None] * out_back)
        product = lax.optimization_barrier(jnp.sum(flat_cotangent[token_ids].astype(jnp.float32) * out_back, axis=1))
        gradient = gradient.at[pair_ids].add(jnp.where(is_live, product, jnp.float32(0.0)))
        return ((accumulated, gradient), None)
    start_acc = jnp.zeros((PACK_COUNT * PACK_LENGTH, D), jnp.float32)
    start_grad = jnp.zeros((PACK_COUNT * PACK_LENGTH * TOPK,), jnp.float32)
    (accumulated, gradient), unused = lax.scan(per_expert, (start_acc, start_grad), jnp.arange(EXPERTS))
    layer_out = (hidden_state + accumulated).astype(jnp.bfloat16).reshape(PACK_COUNT, PACK_LENGTH, D)
    gate_grad = gradient.reshape(PACK_COUNT, PACK_LENGTH, TOPK)
    return (layer_out, gate_grad)
```

```python
import math

import jax
import jax.numpy as jnp
from jax import lax
from jax.experimental import pallas as pl
from jax.experimental.pallas import tpu as pltpu
from jax.sharding import PartitionSpec as P

QUERY_HEADS = 32
KEY_VALUE_HEADS = 4
HEAD_SIZE = 128
MAIN = 8
EXTRA = 2
QUARTERS = 4
BF = jnp.bfloat16
F32 = jnp.float32
VMEM_LIMIT = 60 * 1024 * 1024


def dot(a, b):
    return jnp.dot(a, b, preferred_element_type=F32)


def attend_heads(q_heads, k_heads, v_heads, doc_rows):
    length = q_heads.shape[0]
    group = QUERY_HEADS // KEY_VALUE_HEADS
    score_scale = 1.0 / math.sqrt(HEAD_SIZE)
    positions = jnp.arange(length)
    allowed = (positions[None, :] <= positions[:, None]) & (doc_rows[None, :] == doc_rows[:, None])
    query_block = q_heads.reshape(length, group, HEAD_SIZE)
    scores = jnp.einsum("rgd,jd->grj", query_block, k_heads, preferred_element_type=F32) * score_scale
    scores = jnp.where(allowed[None], scores, -jnp.inf)
    row_max = jnp.max(scores, axis=-1, keepdims=True)
    raised = jnp.exp(scores - row_max)
    weights_bf = (raised / jnp.sum(raised, axis=-1, keepdims=True)).astype(BF)
    block_out = jnp.einsum("grj,jd->rgd", weights_bf, v_heads, preferred_element_type=F32)
    return block_out.astype(BF).reshape(length, group * HEAD_SIZE)


def pack_kernel(projected, residual, gain, main_hot, extra_hot, hidden, out, stacked):
    step = pl.program_id(0)
    tokens = residual.shape[0]
    quarter = stacked.shape[1]

    @pl.when(step == 0)
    def _():
        state = residual[...].astype(F32) + projected[...].astype(F32)
        hidden[...] = state
        mean = jnp.mean(state * state, axis=-1, keepdims=True)
        normed = (state / jnp.sqrt(mean + 1e-06) * gain[...]).astype(BF)
        for c in range(QUARTERS):
            stacked[c * tokens : (c + 1) * tokens, :] = normed[:, c * quarter : (c + 1) * quarter]

    @pl.when(step < QUARTERS)
    def _():
        rows = stacked[pl.ds(pl.multiple_of(step * tokens, tokens), tokens), :]
        out[...] = dot(main_hot[...], rows).astype(BF)

    @pl.when(step == QUARTERS)
    def _():
        out[...] = dot(extra_hot[...], stacked[...]).astype(BF)


def pack(projected, residual, gain, main_hot, extra_hot):
    tokens, width = residual.shape
    quarter = width // QUARTERS
    slots = main_hot.shape[0]
    whole = lambda shape: pl.BlockSpec(shape, lambda i: (0, 0))
    return pl.pallas_call(
        pack_kernel,
        grid=(QUARTERS + 1,),
        in_specs=[
            whole((tokens, width)),
            whole((tokens, width)),
            whole((1, width)),
            whole(main_hot.shape),
            whole(extra_hot.shape),
        ],
        out_specs=[whole((tokens, width)), pl.BlockSpec((slots, quarter), lambda i: (0, i))],
        out_shape=[
            jax.ShapeDtypeStruct((tokens, width), F32),
            jax.ShapeDtypeStruct((slots, width + quarter), BF),
        ],
        scratch_shapes=[pltpu.VMEM((QUARTERS * tokens, quarter), BF)],
        compiler_params=pltpu.CompilerParams(vmem_limit_bytes=VMEM_LIMIT),
        name="norm_pack",
    )(projected, residual, gain, main_hot, extra_hot)


def regroup_matrix(transposed):
    size = 32 * QUARTERS * EXTRA
    grouped = lax.broadcasted_iota(jnp.int32, (size, size), 1 if transposed else 0)
    plain = lax.broadcasted_iota(jnp.int32, (size, size), 0 if transposed else 1)
    c, rest = grouped // (32 * EXTRA), grouped % (32 * EXTRA)
    source = (rest // EXTRA) * (QUARTERS * EXTRA) + c * EXTRA + rest % EXTRA
    return (source == plain).astype(F32).astype(BF)


def expert_kernel(main, extra, w_in, w_down, out, acc, act, parts):
    step = pl.program_id(0)
    slots = main.shape[0]
    hidden = act.shape[1]
    extras = parts.shape[1]
    groups = slots // 256
    per = extras // groups

    @pl.when(step == 0)
    def _():
        swap = regroup_matrix(False)
        for g in range(groups):
            rows = dot(swap, extra[g * 256 : (g + 1) * 256, :]).astype(BF)
            for c in range(QUARTERS):
                parts[c, g * per : (g + 1) * per, :] = rows[c * per : (c + 1) * per, :]

    @pl.when(step == 0)
    def _():
        acc[:slots, :] = dot(main[...], w_in[...])
        acc[slots:, :] = dot(parts[0], w_in[...])

    @pl.when((step > 0) & (step < QUARTERS))
    def _():
        acc[:slots, :] += dot(main[...], w_in[...])
        acc[slots:, :] += dot(parts[step], w_in[...])

    @pl.when(step == QUARTERS - 1)
    def _():
        gate = acc[:, :hidden]
        act[...] = (gate / (1.0 + jnp.exp(-gate)) * acc[:, hidden:]).astype(BF)

    @pl.when((step >= QUARTERS) & (step < 2 * QUARTERS))
    def _():
        out[...] = dot(act[:slots, :], w_down[...]).astype(BF)
        parts[step - QUARTERS] = dot(act[slots:, :], w_down[...]).astype(BF)

    @pl.when(step == 2 * QUARTERS)
    def _():
        swap = regroup_matrix(True)
        for g in range(groups):
            rows = jnp.concatenate([parts[c, g * per : (g + 1) * per, :] for c in range(QUARTERS)], axis=0)
            out[g * 256 : (g + 1) * 256, :] = dot(swap, rows).astype(BF)


def run_expert(incoming, w_in, w_down):
    slots = incoming.shape[0]
    width = w_in.shape[0]
    hidden = w_down.shape[0]
    quarter = width // QUARTERS
    extras = slots // MAIN * EXTRA
    last = QUARTERS - 1
    return pl.pallas_call(
        expert_kernel,
        grid=(2 * QUARTERS + 1,),
        in_specs=[
            pl.BlockSpec((slots, quarter), lambda i: (0, jnp.minimum(i, last))),
            pl.BlockSpec((slots, quarter), lambda i: (0, QUARTERS)),
            pl.BlockSpec((quarter, 2 * hidden), lambda i: (jnp.minimum(i, last), 0)),
            pl.BlockSpec((hidden, quarter), lambda i: (0, jnp.clip(i - QUARTERS, 0, last))),
        ],
        out_specs=pl.BlockSpec((slots, quarter), lambda i: (0, jnp.maximum(i - QUARTERS, 0))),
        out_shape=jax.ShapeDtypeStruct((slots, width + quarter), BF),
        scratch_shapes=[
            pltpu.VMEM((slots + extras, 2 * hidden), F32),
            pltpu.VMEM((slots + extras, hidden), BF),
            pltpu.VMEM((QUARTERS, extras, quarter), BF),
        ],
        compiler_params=pltpu.CompilerParams(vmem_limit_bytes=VMEM_LIMIT),
        name="experts",
    )(incoming, incoming, w_in, w_down)


def combine_kernel(main, extra, hidden, cot, gates_main, gates_extra, keys_main, keys_extra, out, grad, dots_main, dots_extra):
    step = pl.program_id(0)
    tokens = hidden.shape[0]
    slots = main.shape[0]
    of_quarter = lax.broadcasted_iota(jnp.int32, (1, slots), 1) % (QUARTERS * EXTRA) // EXTRA == step
    from_main = dot(gates_main[...], main[...])
    weights = jnp.where(of_quarter, gates_extra[...].astype(F32), 0.0).astype(BF)
    from_extra = dot(weights, extra[...])
    mixed = hidden[...] + (from_main[:tokens] + from_main[tokens:] + from_extra[:tokens] + from_extra[tokens:])
    out[...] = mixed.astype(BF)
    contract_last = (((1,), (1,)), ((), ()))
    new_main = lax.dot_general(cot[...], main[...], contract_last, preferred_element_type=F32)
    new_extra = lax.dot_general(cot[...], extra[...], contract_last, preferred_element_type=F32)
    new_extra = jnp.where(of_quarter, new_extra, 0.0)

    @pl.when(step == 0)
    def _():
        dots_main[...] = new_main
        dots_extra[...] = new_extra

    @pl.when(step > 0)
    def _():
        dots_main[...] += new_main
        dots_extra[...] += new_extra

    @pl.when(step == QUARTERS - 1)
    def _():
        slot = lax.broadcasted_iota(jnp.int32, (tokens, slots), 1)
        extra_slot = slot // (QUARTERS * EXTRA) * EXTRA + slot % EXTRA
        sums = []
        for k in range(keys_main.shape[1]):
            picked = jnp.where(slot == keys_main[:, k : k + 1], dots_main[...], 0.0)
            picked += jnp.where(extra_slot == keys_extra[:, k : k + 1], dots_extra[...], 0.0)
            sums.append(jnp.sum(picked, axis=1, keepdims=True))
        grad[...] = jnp.concatenate(sums, axis=1)


def combine(returned, hidden, cot, gates_main, gates_extra, keys_main, keys_extra):
    slots = returned.shape[0]
    tokens, width = hidden.shape
    quarter = width // QUARTERS
    top = keys_main.shape[1]
    whole = lambda shape: pl.BlockSpec(shape, lambda i: (0, 0))
    part = lambda shape: pl.BlockSpec(shape, lambda i: (0, i))
    return pl.pallas_call(
        combine_kernel,
        grid=(QUARTERS,),
        in_specs=[
            part((slots, quarter)),
            pl.BlockSpec((slots, quarter), lambda i: (0, QUARTERS)),
            part((tokens, quarter)),
            part((tokens, quarter)),
            whole(gates_main.shape),
            whole(gates_extra.shape),
            whole(keys_main.shape),
            whole(keys_extra.shape),
        ],
        out_specs=[part((tokens, quarter)), whole((tokens, top))],
        out_shape=[jax.ShapeDtypeStruct((tokens, width), BF), jax.ShapeDtypeStruct((tokens, top), F32)],
        scratch_shapes=[pltpu.VMEM((tokens, slots), F32), pltpu.VMEM((tokens, slots), F32)],
        compiler_params=pltpu.CompilerParams(vmem_limit_bytes=VMEM_LIMIT),
        name="combine",
    )(returned, returned, hidden, cot, gates_main, gates_extra, keys_main, keys_extra)


def split_in_two(values):
    high = values.astype(BF)
    return jnp.concatenate([high, (values - high.astype(F32)).astype(BF)], axis=0)


def routing(chosen, gates, experts):
    tokens = chosen.shape[0]
    hits = chosen[:, :, None] == jnp.arange(experts, dtype=jnp.int32)[None, None, :]
    member = jnp.any(hits, axis=1)
    earlier = jnp.arange(tokens)[None, :] < jnp.arange(tokens)[:, None]
    rank = dot(earlier.astype(BF), member.astype(BF)).astype(jnp.int32)
    rank = jnp.where(member, rank, -1)
    gate_of = jnp.sum(jnp.where(hits, gates[:, :, None], 0.0), axis=1)
    pair_rank = jnp.sum(jnp.where(hits, rank[:, None, :], 0), axis=2)

    is_main = rank[:, :, None] == jnp.arange(MAIN, dtype=jnp.int32)
    extra_row = jnp.arange(QUARTERS * EXTRA, dtype=jnp.int32)
    is_extra = rank[:, :, None] == MAIN + extra_row % EXTRA
    main_hot = is_main.astype(BF).transpose(1, 2, 0).reshape(experts * MAIN, tokens)
    in_quarter = extra_row[None, :, None, None] // EXTRA == jnp.arange(QUARTERS)[None, None, :, None]
    extra_hot = (is_extra.transpose(1, 2, 0)[:, :, None, :] & in_quarter).astype(BF)
    extra_hot = extra_hot.reshape(experts * QUARTERS * EXTRA, QUARTERS * tokens)

    gates_main = jnp.where(is_main, gate_of[:, :, None], 0.0).reshape(tokens, experts * MAIN)
    gates_extra = jnp.where(is_extra, gate_of[:, :, None], 0.0).reshape(tokens, experts * QUARTERS * EXTRA)
    keys_main = jnp.where(pair_rank < MAIN, chosen * MAIN + pair_rank, -1)
    keys_extra = jnp.where(pair_rank >= MAIN, chosen * EXTRA + pair_rank - MAIN, -1)
    return main_hot, extra_hot, split_in_two(gates_main), split_in_two(gates_extra), keys_main, keys_extra


def shards(
    queries,
    rotated_keys,
    projected_values,
    doc_ids,
    residual,
    out_weight,
    norm_gain,
    routes,
    gate_vals,
    cotangent,
    expert_in,
    expert_down,
):
    seq_count = lax.axis_size("seq")
    experts = seq_count * lax.axis_size("exp")
    tokens, width = residual.shape[1:]
    full_rows = lax.all_gather(out_weight, "exp", axis=1, tiled=True)

    by_head = lambda a: a[0].reshape(tokens, seq_count, -1)
    heads = jnp.concatenate([by_head(queries), by_head(rotated_keys), by_head(projected_values)], axis=2)
    heads = lax.all_to_all(heads.transpose(1, 0, 2), "seq", split_axis=0, concat_axis=0, tiled=True)
    heads = heads.reshape(seq_count * tokens, -1)
    q_width = width // seq_count
    attended = attend_heads(
        heads[:, :q_width],
        heads[:, q_width : q_width + HEAD_SIZE],
        heads[:, q_width + HEAD_SIZE :],
        doc_ids[0],
    )
    partial = dot(attended, full_rows).astype(BF)
    projected = lax.psum_scatter(partial, "seq", scatter_dimension=0, tiled=True)

    main_hot, extra_hot, gates_main, gates_extra, keys_main, keys_extra = routing(routes[0], gate_vals[0], experts)
    hidden, outgoing = pack(projected, residual[0], norm_gain[None, :], main_hot, extra_hot)

    def exchange(slots):
        blocks = slots.reshape(experts, MAIN, slots.shape[1])
        blocks = lax.all_to_all(blocks, ("seq", "exp"), split_axis=0, concat_axis=0, tiled=True)
        return blocks.reshape(slots.shape)

    results = run_expert(exchange(outgoing), expert_in[0], expert_down[0])
    layer_out, gate_grad = combine(
        exchange(results), hidden, cotangent[0], gates_main, gates_extra, keys_main, keys_extra
    )
    return layer_out[None], gate_grad[None]


def solution(mesh):
    in_specs = (
        P("exp", "seq", None),
        P("exp", "seq", None),
        P("exp", "seq", None),
        P("exp", None),
        P("exp", "seq", None),
        P("seq", "exp"),
        P(),
        P("exp", "seq", None),
        P("exp", "seq", None),
        P("exp", "seq", None),
        P(("seq", "exp"), None, None),
        P(("seq", "exp"), None, None),
    )
    out_specs = (P("exp", "seq", None), P("exp", "seq", None))
    return jax.shard_map(shards, mesh=mesh, in_specs=in_specs, out_specs=out_specs, check_vma=False)
```

```python
import math

import jax
import jax.numpy as jnp
from jax import lax
from jax.experimental import pallas as pl
from jax.experimental.pallas import tpu as pltpu
from jax.sharding import PartitionSpec as P

QUERY_HEADS = 32
KEY_VALUE_HEADS = 4
HEAD_SIZE = 128
MAIN = 8
EXTRA = 2
BLOCKS = 4
CHUNKS = 2
BF = jnp.bfloat16
F32 = jnp.float32
PARAMS = pltpu.CompilerParams(vmem_limit_bytes=60 * 1024 * 1024)


def dot(a, b):
    return jnp.dot(a, b, preferred_element_type=F32)


def whole(shape):
    return pl.BlockSpec(shape, lambda i, *_: (0,) * len(shape))


def columns(rows, block, first=0, shift=0, last=BLOCKS - 1):
    return pl.BlockSpec((rows, block), lambda i, *_: (0, first + jnp.clip(i - shift, 0, last)))


def attend_heads(q_heads, k_heads, v_heads, doc_rows):
    length = q_heads.shape[0]
    group = QUERY_HEADS // KEY_VALUE_HEADS
    score_scale = 1.0 / math.sqrt(HEAD_SIZE)
    positions = jnp.arange(length)
    allowed = (positions[None, :] <= positions[:, None]) & (doc_rows[None, :] == doc_rows[:, None])
    query_block = q_heads.reshape(length, group, HEAD_SIZE)
    scores = jnp.einsum("rgd,jd->grj", query_block, k_heads, preferred_element_type=F32) * score_scale
    scores = jnp.where(allowed[None], scores, -jnp.inf)
    row_max = jnp.max(scores, axis=-1, keepdims=True)
    raised = jnp.exp(scores - row_max)
    weights_bf = (raised / jnp.sum(raised, axis=-1, keepdims=True)).astype(BF)
    block_out = jnp.einsum("grj,jd->rgd", weights_bf, v_heads, preferred_element_type=F32)
    return block_out.astype(BF).reshape(length, group * HEAD_SIZE)


def project_kernel(place, attended, weight, own, *rest):
    sends, result = rest[:-1], rest[-1]
    tokens = own.shape[0]
    count = len(sends) + 1
    result[...] = dot(attended[...], weight[...])

    def rows(shift):
        start = lax.rem(place[0] + shift, count) * tokens
        return result[pl.ds(pl.multiple_of(start, tokens), tokens), :]

    own[...] = rows(0)
    for shift, send in enumerate(sends, 1):
        send[...] = rows(shift).astype(BF)


def project(place, attended, weight, chunk, count):
    length, inner = attended.shape
    tokens = length // count
    width = weight.shape[1] // CHUNKS
    block = width // BLOCKS
    return pl.pallas_call(
        project_kernel,
        grid_spec=pltpu.PrefetchScalarGridSpec(
            num_scalar_prefetch=1,
            grid=(BLOCKS,),
            in_specs=[whole((length, inner)), columns(inner, block, chunk * BLOCKS)],
            out_specs=[columns(tokens, block)] * count,
            scratch_shapes=[pltpu.VMEM((length, block), F32)],
        ),
        out_shape=[jax.ShapeDtypeStruct((tokens, width), F32)]
        + [jax.ShapeDtypeStruct((tokens, width), BF)] * (count - 1),
        compiler_params=PARAMS,
        name=f"project_{chunk}",
    )(place, attended, weight)


def pack_kernel(*refs):
    *sums, residual, gain, main_hot, extra_hot, hidden, out, stacked = refs
    step = pl.program_id(0)
    tokens = residual.shape[0]

    @pl.when(step < BLOCKS)
    def _():
        state = residual[...].astype(F32)
        for part in sums:
            state += part[...].astype(F32)
        hidden[...] = state
        rows = (state * gain[...]).astype(BF)
        stacked[pl.ds(pl.multiple_of(step * tokens, tokens), tokens), :] = rows
        out[...] = dot(main_hot[...], rows).astype(BF)

    @pl.when(step == BLOCKS)
    def _():
        out[...] = dot(extra_hot[...], stacked[...]).astype(BF)


def pack(sums, residual, gain, main_hot, extra_hot, chunk):
    tokens, full = residual.shape
    width = full // CHUNKS
    block = width // BLOCKS
    slots = main_hot.shape[0]
    return pl.pallas_call(
        pack_kernel,
        grid=(BLOCKS + 1,),
        in_specs=[columns(tokens, block)] * len(sums)
        + [
            columns(tokens, block, chunk * BLOCKS),
            columns(1, block, chunk * BLOCKS),
            whole(main_hot.shape),
            whole(extra_hot.shape),
        ],
        out_specs=[columns(tokens, block), columns(slots, block, last=BLOCKS)],
        out_shape=[
            jax.ShapeDtypeStruct((tokens, width), F32),
            jax.ShapeDtypeStruct((slots, width + block), BF),
        ],
        scratch_shapes=[pltpu.VMEM((BLOCKS * tokens, block), BF)],
        compiler_params=PARAMS,
        name=f"pack_{chunk}",
    )(*sums, residual, gain, main_hot, extra_hot)


def regroup_matrix(transposed):
    size = 32 * BLOCKS * EXTRA
    grouped = lax.broadcasted_iota(jnp.int32, (size, size), 1 if transposed else 0)
    plain = lax.broadcasted_iota(jnp.int32, (size, size), 0 if transposed else 1)
    c, rest = grouped // (32 * EXTRA), grouped % (32 * EXTRA)
    source = (rest // EXTRA) * (BLOCKS * EXTRA) + c * EXTRA + rest % EXTRA
    return (source == plain).astype(F32).astype(BF)


def regroup(extra, parts):
    size = 32 * BLOCKS * EXTRA
    per = 32 * EXTRA
    swap = regroup_matrix(False)
    for g in range(extra.shape[0] // size):
        rows = dot(swap, extra[g * size : (g + 1) * size, :]).astype(BF)
        for c in range(BLOCKS):
            parts[c, g * per : (g + 1) * per, :] = rows[c * per : (c + 1) * per, :]


def ungroup(parts, out):
    size = 32 * BLOCKS * EXTRA
    per = 32 * EXTRA
    swap = regroup_matrix(True)
    for g in range(out.shape[0] // size):
        rows = jnp.concatenate([parts[c, g * per : (g + 1) * per, :] for c in range(BLOCKS)], axis=0)
        out[g * size : (g + 1) * size, :] = dot(swap, rows).astype(BF)


def add_squares(squares, rows, inverse_gain):
    total = None
    for j in range(0, rows.shape[1], 128):
        values = rows[:, j : j + 128].astype(F32) * inverse_gain[:, j : j + 128]
        total = values * values if total is None else total + values * values
    squares[...] += total


def up_step(step, main, extra, inverse_gain, w_in, acc, squares, parts):
    slots = main.shape[0]

    @pl.when(step == 0)
    def _():
        regroup(extra, parts)
        acc[...] = jnp.zeros_like(acc)
        squares[...] = jnp.zeros_like(squares)

    acc[:slots, :] += dot(main[...], w_in[...])
    acc[slots:, :] += dot(parts[step], w_in[...])
    add_squares(squares.at[:slots, :], main, inverse_gain)
    add_squares(squares.at[slots:, :], parts.at[step], inverse_gain)


def first_kernel(main, extra, inverse_gain, w_in, acc, squares, parts):
    up_step(pl.program_id(0), main, extra, inverse_gain, w_in, acc, squares, parts)


def first_half(incoming, inverse_gain, w_in):
    slots = incoming.shape[0]
    block = w_in.shape[0] // CHUNKS // BLOCKS
    extras = slots // MAIN * EXTRA
    return pl.pallas_call(
        first_kernel,
        grid=(BLOCKS,),
        in_specs=[
            columns(slots, block),
            pl.BlockSpec((slots, block), lambda i: (0, BLOCKS)),
            columns(1, block),
            pl.BlockSpec((block, w_in.shape[1]), lambda i: (i, 0)),
        ],
        out_specs=[whole((slots + extras, w_in.shape[1])), whole((slots + extras, 128))],
        out_shape=[
            jax.ShapeDtypeStruct((slots + extras, w_in.shape[1]), F32),
            jax.ShapeDtypeStruct((slots + extras, 128), F32),
        ],
        scratch_shapes=[pltpu.VMEM((BLOCKS, extras, block), BF)],
        compiler_params=PARAMS,
        name="up_0",
    )(incoming, incoming, inverse_gain, w_in)


def down_step(step, act, w_down, out, parts):
    slots = out.shape[0]

    @pl.when(step < BLOCKS)
    def _():
        out[...] = dot(act[:slots, :], w_down[...]).astype(BF)
        parts[step] = dot(act[slots:, :], w_down[...]).astype(BF)

    @pl.when(step == BLOCKS)
    def _():
        ungroup(parts, out)


def second_kernel(main, extra, inverse_gain, w_in, before, squares_before, w_down, act, out, acc, squares, parts, width):
    step = pl.program_id(0)
    hidden = act.shape[1]
    part = before.shape[0]

    @pl.when(step < BLOCKS)
    def _():
        up_step(step, main, extra, inverse_gain, w_in, acc, squares, parts)
        start = pl.multiple_of(step * part, part)
        acc[pl.ds(start, part), :] += before[...]

    @pl.when(step == BLOCKS - 1)
    def _():
        @pl.loop(0, act.shape[0] // 128)
        def _(r):
            rows = pl.ds(pl.multiple_of(r * 128, 128), 128)
            total = jnp.sum(squares[rows, :] + squares_before[rows, :], axis=1, keepdims=True)
            scale = 1.0 / jnp.sqrt(total * (1.0 / width) + 1e-06)
            gate = acc[rows, :hidden] * scale
            act[rows, :] = (gate / (1.0 + jnp.exp(-gate)) * (acc[rows, hidden:] * scale)).astype(BF)

    @pl.when(step >= BLOCKS)
    def _():
        down_step(step - BLOCKS, act, w_down, out, parts)


def second_half(incoming, inverse_gain, w_in, before, squares, w_down):
    slots = incoming.shape[0]
    width, both = w_in.shape
    hidden = w_down.shape[0]
    chunk = width // CHUNKS
    block = chunk // BLOCKS
    rows = before.shape[0]
    last = BLOCKS - 1

    def kernel(*refs):
        second_kernel(*refs, width)

    return pl.pallas_call(
        kernel,
        grid=(2 * BLOCKS + 1,),
        in_specs=[
            columns(slots, block),
            pl.BlockSpec((slots, block), lambda i: (0, BLOCKS)),
            columns(1, block, BLOCKS),
            pl.BlockSpec((block, both), lambda i: (BLOCKS + jnp.minimum(i, last), 0)),
            pl.BlockSpec((rows // BLOCKS, both), lambda i: (jnp.minimum(i, last), 0)),
            whole((rows, 128)),
            columns(hidden, block, shift=BLOCKS),
        ],
        out_specs=[whole((rows, hidden)), columns(slots, block, shift=BLOCKS, last=BLOCKS)],
        out_shape=[
            jax.ShapeDtypeStruct((rows, hidden), BF),
            jax.ShapeDtypeStruct((slots, chunk + block), BF),
        ],
        scratch_shapes=[
            pltpu.VMEM((rows, both), F32),
            pltpu.VMEM((rows, 128), F32),
            pltpu.VMEM((BLOCKS, rows - slots, block), BF),
        ],
        compiler_params=PARAMS,
        name="up_1",
    )(incoming, incoming, inverse_gain, w_in, before, squares, w_down)


def down_kernel(act, w_down, out, parts):
    down_step(pl.program_id(0), act, w_down, out, parts)


def down(act, w_down, slots):
    rows, hidden = act.shape
    chunk = w_down.shape[1] // CHUNKS
    block = chunk // BLOCKS
    return pl.pallas_call(
        down_kernel,
        grid=(BLOCKS + 1,),
        in_specs=[whole((rows, hidden)), columns(hidden, block, BLOCKS)],
        out_specs=columns(slots, block, last=BLOCKS),
        out_shape=jax.ShapeDtypeStruct((slots, chunk + block), BF),
        scratch_shapes=[pltpu.VMEM((BLOCKS, rows - slots, block), BF)],
        compiler_params=PARAMS,
        name="down_1",
    )(act, w_down)


def combine_step(main, extra, hidden, cot, gates_main, gates_extra, out, dots_main, dots_extra, parts):
    step = pl.program_id(0)
    tokens = hidden.shape[0]

    @pl.when(step == 0)
    def _():
        regroup(extra, parts)

    rows = parts[step]
    both = dot(gates_main[...], main[...]) + dot(gates_extra[...], rows)
    out[...] = (hidden[...] + (both[:tokens] + both[tokens:])).astype(BF)
    contract_last = (((1,), (1,)), ((), ()))
    dots_main[...] += lax.dot_general(cot[...], main[...], contract_last, preferred_element_type=F32)
    dots_extra[...] += lax.dot_general(cot[...], rows, contract_last, preferred_element_type=F32)


def combine_first(main, extra, hidden, cot, gates_main, gates_extra, out, dots_main, dots_extra, parts):
    @pl.when(pl.program_id(0) == 0)
    def _():
        dots_main[...] = jnp.zeros_like(dots_main)
        dots_extra[...] = jnp.zeros_like(dots_extra)

    combine_step(main, extra, hidden, cot, gates_main, gates_extra, out, dots_main, dots_extra, parts)


def combine_last(
    main, extra, hidden, cot, gates_main, gates_extra, old_main, old_extra, keys_main, keys_extra, before,
    out, grad, parts, dots_main, dots_extra,
):
    @pl.when(pl.program_id(0) == 0)
    def _():
        dots_main[...] = old_main[...]
        dots_extra[...] = old_extra[...]

    combine_step(main, extra, hidden, cot, gates_main, gates_extra, out, dots_main, dots_extra, parts)

    @pl.when(pl.program_id(0) == BLOCKS - 1)
    def _():
        main_slot = lax.broadcasted_iota(jnp.int32, dots_main.shape, 1)
        extra_slot = lax.broadcasted_iota(jnp.int32, dots_extra.shape, 1)
        sums = []
        for k in range(keys_main.shape[1]):
            in_main = jnp.where(main_slot == keys_main[:, k : k + 1], dots_main[...], 0.0)
            in_extra = jnp.where(extra_slot == keys_extra[:, k : k + 1], dots_extra[...], 0.0)
            sums.append(jnp.sum(in_main, axis=1, keepdims=True) + jnp.sum(in_extra, axis=1, keepdims=True))
        grad[...] = jnp.concatenate(sums, axis=1)


def combine(returned, hidden, cot, gates_main, gates_extra, chunk, more=None):
    slots = returned.shape[0]
    tokens, full = cot.shape
    block = full // CHUNKS // BLOCKS
    extras = gates_extra.shape[1]
    here = chunk * BLOCKS
    args = [returned, returned, hidden, cot, gates_main, gates_extra]
    in_specs = [
        columns(slots, block),
        pl.BlockSpec((slots, block), lambda i: (0, BLOCKS)),
        columns(tokens, block),
        columns(tokens, block, here),
        whole(gates_main.shape),
        whole(gates_extra.shape),
    ]
    out_specs = [columns(tokens, block, here)]
    out_shape = [jax.ShapeDtypeStruct((tokens, full), BF)]
    scratch = [pltpu.VMEM((BLOCKS, extras, block), BF)]
    aliases = {}
    if more is None:
        out_specs += [whole((tokens, slots)), whole((tokens, extras))]
        out_shape += [jax.ShapeDtypeStruct((tokens, slots), F32), jax.ShapeDtypeStruct((tokens, extras), F32)]
    else:
        args += more
        in_specs += [whole(a.shape) for a in more[:-1]] + [pl.BlockSpec(memory_space=pl.ANY)]
        top = more[2].shape[1]
        out_specs += [whole((tokens, top))]
        out_shape += [jax.ShapeDtypeStruct((tokens, top), F32)]
        scratch += [pltpu.VMEM((tokens, slots), F32), pltpu.VMEM((tokens, extras), F32)]
        aliases = {len(args) - 1: 0}
    return pl.pallas_call(
        combine_first if more is None else combine_last,
        grid=(BLOCKS,),
        in_specs=in_specs,
        out_specs=out_specs,
        out_shape=out_shape,
        scratch_shapes=scratch,
        input_output_aliases=aliases,
        compiler_params=PARAMS,
        name=f"combine_{chunk}",
    )(*args)


def split_in_two(values):
    high = values.astype(BF)
    return jnp.concatenate([high, (values - high.astype(F32)).astype(BF)], axis=0)


def routing(chosen, gates, experts):
    tokens = chosen.shape[0]
    hits = chosen[:, :, None] == jnp.arange(experts, dtype=jnp.int32)[None, None, :]
    member = jnp.any(hits, axis=1)
    earlier = jnp.arange(tokens)[None, :] < jnp.arange(tokens)[:, None]
    rank = dot(earlier.astype(BF), member.astype(BF)).astype(jnp.int32)
    rank = jnp.where(member, rank, -1)
    gate_of = jnp.sum(jnp.where(hits, gates[:, :, None], 0.0), axis=1)
    pair_rank = jnp.sum(jnp.where(hits, rank[:, None, :], 0), axis=2)

    def slots_of(first, count):
        return rank[:, :, None] == first + jnp.arange(count, dtype=jnp.int32)

    is_main, is_extra = slots_of(0, MAIN), slots_of(MAIN, EXTRA)
    main_hot = is_main.astype(BF).transpose(1, 2, 0).reshape(experts * MAIN, tokens)
    extra_row = jnp.arange(BLOCKS * EXTRA, dtype=jnp.int32)
    extra_rows = rank[:, :, None] == MAIN + extra_row % EXTRA
    in_block = extra_row[None, :, None, None] // EXTRA == jnp.arange(BLOCKS)[None, None, :, None]
    extra_hot = (extra_rows.transpose(1, 2, 0)[:, :, None, :] & in_block).astype(BF)
    extra_hot = extra_hot.reshape(experts * BLOCKS * EXTRA, BLOCKS * tokens)

    def gates_in(mask):
        return split_in_two(jnp.where(mask, gate_of[:, :, None], 0.0).reshape(tokens, -1))

    keys_main = jnp.where(pair_rank < MAIN, chosen * MAIN + pair_rank, -1)
    keys_extra = jnp.where(pair_rank >= MAIN, chosen * EXTRA + pair_rank - MAIN, -1)
    return main_hot, extra_hot, gates_in(is_main), gates_in(is_extra), keys_main, keys_extra


def shards(
    queries,
    rotated_keys,
    projected_values,
    doc_ids,
    residual,
    out_weight,
    norm_gain,
    routes,
    gate_vals,
    cotangent,
    expert_in,
    expert_down,
):
    seq_count = lax.axis_size("seq")
    experts = seq_count * lax.axis_size("exp")
    tokens, width = residual.shape[1:]
    full_rows = lax.all_gather(out_weight, "exp", axis=1, tiled=True)

    by_head = lambda a: a[0].reshape(tokens, seq_count, -1)
    heads = jnp.concatenate([by_head(queries), by_head(rotated_keys), by_head(projected_values)], axis=2)
    heads = lax.all_to_all(heads.transpose(1, 0, 2), "seq", split_axis=0, concat_axis=0, tiled=True)
    heads = heads.reshape(seq_count * tokens, -1)
    q_width = width // seq_count
    attended = attend_heads(
        heads[:, :q_width],
        heads[:, q_width : q_width + HEAD_SIZE],
        heads[:, q_width + HEAD_SIZE :],
        doc_ids[0],
    )
    place = lax.axis_index("seq").astype(jnp.int32)[None]

    def project_and_send(chunk):
        own, *sends = project(place, attended, full_rows, chunk, seq_count)
        arrived = [
            lax.ppermute(send, "seq", [(i, (i + shift) % seq_count) for i in range(seq_count)])
            for shift, send in enumerate(sends, 1)
        ]
        return [own, *arrived]

    def exchange(slots):
        blocks = slots.reshape(experts, MAIN, slots.shape[1])
        blocks = lax.all_to_all(blocks, ("seq", "exp"), split_axis=0, concat_axis=0, tiled=True)
        return blocks.reshape(slots.shape)

    main_hot, extra_hot, gates_main, gates_extra, keys_main, keys_extra = routing(routes[0], gate_vals[0], experts)
    gain = norm_gain[None, :]
    inverse_gain = 1.0 / gain
    sums = [project_and_send(c) for c in range(CHUNKS)]
    hidden, outgoing = zip(*[pack(sums[c], residual[0], gain, main_hot, extra_hot, c) for c in range(CHUNKS)])
    incoming = [exchange(o) for o in outgoing]
    before, squares = first_half(incoming[0], inverse_gain, expert_in[0])
    act, results = second_half(incoming[1], inverse_gain, expert_in[0], before, squares, expert_down[0])
    returned = exchange(results)
    results = down(act, expert_down[0], results.shape[0])
    later = exchange(results)
    cot = cotangent[0]
    layer_out, *dots = combine(returned, hidden[0], cot, gates_main, gates_extra, 0)
    more = [*dots, keys_main, keys_extra, layer_out]
    layer_out, gate_grad = combine(later, hidden[1], cot, gates_main, gates_extra, 1, more)
    return layer_out[None], gate_grad[None]


def solution(mesh):
    in_specs = (
        P("exp", "seq", None),
        P("exp", "seq", None),
        P("exp", "seq", None),
        P("exp", None),
        P("exp", "seq", None),
        P("seq", "exp"),
        P(),
        P("exp", "seq", None),
        P("exp", "seq", None),
        P("exp", "seq", None),
        P(("seq", "exp"), None, None),
        P(("seq", "exp"), None, None),
    )
    out_specs = (P("exp", "seq", None), P("exp", "seq", None))
    return jax.shard_map(shards, mesh=mesh, in_specs=in_specs, out_specs=out_specs, check_vma=False)
```

```python
import functools
import math

import jax
import jax.numpy as jnp
from jax import lax
from jax.experimental import pallas as pl
from jax.experimental.pallas import tpu as pltpu
from jax.sharding import PartitionSpec as P

QUERY_HEADS = 32
KEY_VALUE_HEADS = 4
HEAD_SIZE = 128
MAIN = 8
EXTRA = 2
BLOCKS = 4
CHUNKS = 2
BF = jnp.bfloat16
F32 = jnp.float32
LAST = (((1,), (1,)), ((), ()))
PARAMS = pltpu.CompilerParams(vmem_limit_bytes=60 * 1024 * 1024)


def dot(a, b):
    return jnp.dot(a, b, preferred_element_type=F32)


def whole(shape):
    return pl.BlockSpec(shape, lambda i, *_: (0,) * len(shape))


def columns(rows, block, first=0, shift=0, last=BLOCKS - 1):
    return pl.BlockSpec((rows, block), lambda i, *_: (0, first + jnp.clip(i - shift, 0, last)))


def attend_heads(q_heads, k_heads, v_heads, doc_rows):
    length = q_heads.shape[0]
    group = QUERY_HEADS // KEY_VALUE_HEADS
    score_scale = 1.0 / math.sqrt(HEAD_SIZE)
    positions = jnp.arange(length)
    allowed = (positions[None, :] <= positions[:, None]) & (doc_rows[None, :] == doc_rows[:, None])
    query_block = q_heads.reshape(length, group, HEAD_SIZE)
    scores = jnp.einsum("rgd,jd->grj", query_block, k_heads, preferred_element_type=F32) * score_scale
    scores = jnp.where(allowed[None], scores, -jnp.inf)
    row_max = jnp.max(scores, axis=-1, keepdims=True)
    raised = jnp.exp(scores - row_max)
    weights_bf = (raised / jnp.sum(raised, axis=-1, keepdims=True)).astype(BF)
    block_out = jnp.einsum("grj,jd->rgd", weights_bf, v_heads, preferred_element_type=F32)
    return block_out.astype(BF).reshape(length, group * HEAD_SIZE)


def project_kernel(place, attended, weight, own, *rest):
    sends, result = rest[:-1], rest[-1]
    tokens = own.shape[0]
    count = len(sends) + 1
    result[...] = lax.dot_general(attended[...], weight[...], LAST, preferred_element_type=F32)

    def rows(shift):
        start = lax.rem(place[0] + shift, count) * tokens
        return result[pl.ds(pl.multiple_of(start, tokens), tokens), :]

    own[...] = rows(0)
    for shift, send in enumerate(sends, 1):
        send[...] = rows(shift).astype(BF)


def project(place, attended, weight, count):
    length, inner = attended.shape
    tokens = length // count
    width = weight.shape[0]
    block = width // BLOCKS
    return pl.pallas_call(
        project_kernel,
        grid_spec=pltpu.PrefetchScalarGridSpec(
            num_scalar_prefetch=1,
            grid=(BLOCKS,),
            in_specs=[whole((length, inner)), pl.BlockSpec((block, inner), lambda i, *_: (i, 0))],
            out_specs=[columns(tokens, block)] * count,
            scratch_shapes=[pltpu.VMEM((length, block), F32)],
        ),
        out_shape=[jax.ShapeDtypeStruct((tokens, width), F32)]
        + [jax.ShapeDtypeStruct((tokens, width), BF)] * (count - 1),
        compiler_params=PARAMS,
    )(place, attended, weight)


def pack_kernel(count, *refs):
    sums = refs[:count]
    residual, gain, main_hot, extra_hot = refs[count : count + 4]
    hidden, out, stacked = refs[-3:]
    step = pl.program_id(0)
    tokens = residual.shape[0]

    @pl.when(step < BLOCKS)
    def _():
        state = residual[...].astype(F32)
        for part in sums:
            state += part[...].astype(F32)
        hidden[...] = state
        rows = (state * gain[...]).astype(BF)
        stacked[pl.ds(pl.multiple_of(step * tokens, tokens), tokens), :] = rows
        out[...] = dot(main_hot[...], rows).astype(BF)

    @pl.when(step == BLOCKS)
    def _():
        out[...] = dot(extra_hot[...], stacked[...]).astype(BF)


def pack(sums, residual, gain, main_hot, extra_hot, after=()):
    tokens, width = residual.shape
    block = width // BLOCKS
    slots = main_hot.shape[0]
    return pl.pallas_call(
        functools.partial(pack_kernel, len(sums)),
        grid=(BLOCKS + 1,),
        in_specs=[columns(tokens, block)] * len(sums)
        + [
            columns(tokens, block),
            columns(1, block),
            whole(main_hot.shape),
            whole(extra_hot.shape),
        ]
        + [pl.BlockSpec(memory_space=pl.ANY)] * len(after),
        out_specs=[columns(tokens, block), columns(slots, block, last=BLOCKS)],
        out_shape=[
            jax.ShapeDtypeStruct((tokens, width), F32),
            jax.ShapeDtypeStruct((slots, width + block), BF),
        ],
        scratch_shapes=[pltpu.VMEM((BLOCKS * tokens, block), BF)],
        compiler_params=PARAMS,
    )(*sums, residual, gain, main_hot, extra_hot, *after)


def regroup_matrix(transposed):
    size = 32 * BLOCKS * EXTRA
    grouped = lax.broadcasted_iota(jnp.int32, (size, size), 1 if transposed else 0)
    plain = lax.broadcasted_iota(jnp.int32, (size, size), 0 if transposed else 1)
    c, rest = grouped // (32 * EXTRA), grouped % (32 * EXTRA)
    source = (rest // EXTRA) * (BLOCKS * EXTRA) + c * EXTRA + rest % EXTRA
    return (source == plain).astype(F32).astype(BF)


def regroup(extra, parts):
    size = 32 * BLOCKS * EXTRA
    per = 32 * EXTRA
    swap = regroup_matrix(False)
    for g in range(extra.shape[0] // size):
        rows = dot(swap, extra[g * size : (g + 1) * size, :]).astype(BF)
        for c in range(BLOCKS):
            parts[c, g * per : (g + 1) * per, :] = rows[c * per : (c + 1) * per, :]


def ungroup(parts, out):
    size = 32 * BLOCKS * EXTRA
    per = 32 * EXTRA
    swap = regroup_matrix(True)
    for g in range(out.shape[0] // size):
        rows = jnp.concatenate([parts[c, g * per : (g + 1) * per, :] for c in range(BLOCKS)], axis=0)
        out[g * size : (g + 1) * size, :] = dot(swap, rows).astype(BF)


def add_squares(squares, rows, inverse_gain):
    @pl.loop(0, rows.shape[0] // 64)
    def _(r):
        here = pl.ds(pl.multiple_of(r * 64, 64), 64)
        total = squares[here, :]
        for j in range(0, rows.shape[1], 128):
            values = rows[here, j : j + 128].astype(F32) * inverse_gain[:, j : j + 128]
            total += values * values
        squares[here, :] = total


def up_step(step, main, extra, inverse_gain, w_in, acc, squares, parts):
    slots = main.shape[0]
    rows_in = w_in[...].reshape(main.shape[1], w_in.shape[-1])

    @pl.when(step == 0)
    def _():
        regroup(extra, parts)
        acc[...] = jnp.zeros_like(acc)
        squares[...] = jnp.zeros_like(squares)

    acc[:slots, :] += dot(main[...], rows_in)
    acc[slots:, :] += dot(parts[step], rows_in)
    add_squares(squares.at[:slots, :], main, inverse_gain)
    add_squares(squares.at[slots:, :], parts.at[step], inverse_gain)


def weight_blocks(w_in, chunk):
    shards_in, _, rows, both = w_in.shape
    last = BLOCKS - 1
    return pl.BlockSpec(
        (shards_in // BLOCKS, pl.Squeezed(), rows, both), lambda i: (jnp.minimum(i, last), chunk, 0, 0)
    )


def first_kernel(main, extra, inverse_gain, w_in, acc, squares, parts):
    up_step(pl.program_id(0), main, extra, inverse_gain, w_in, acc, squares, parts)


def first_half(incoming, inverse_gain, w_in):
    slots = incoming.shape[0]
    block = inverse_gain.shape[1] // BLOCKS
    extras = slots // MAIN * EXTRA
    both = w_in.shape[-1]
    return pl.pallas_call(
        first_kernel,
        grid=(BLOCKS,),
        in_specs=[
            columns(slots, block),
            pl.BlockSpec((slots, block), lambda i: (0, BLOCKS)),
            columns(1, block),
            weight_blocks(w_in, 0),
        ],
        out_specs=[whole((slots + extras, both)), whole((slots + extras, 128))],
        out_shape=[
            jax.ShapeDtypeStruct((slots + extras, both), F32),
            jax.ShapeDtypeStruct((slots + extras, 128), F32),
        ],
        scratch_shapes=[pltpu.VMEM((BLOCKS, extras, block), BF)],
        compiler_params=PARAMS,
        name="up_0",
    )(incoming, incoming, inverse_gain, w_in)


def second_kernel(main, extra, inverse_gain, w_in, before, squares_before, w_down, out, acc, squares, parts, act, down):
    step = pl.program_id(0)
    slots = main.shape[0]
    hidden = act.shape[1]
    part = before.shape[0]
    width = w_down.shape[1] * BLOCKS

    @pl.when(step < BLOCKS)
    def _():
        up_step(step, main, extra, inverse_gain, w_in, acc, squares, parts)
        start = pl.multiple_of(step * part, part)
        acc[pl.ds(start, part), :] += before[...]

    @pl.when(step == BLOCKS - 1)
    def _():
        @pl.loop(0, act.shape[0] // 128)
        def _(r):
            rows = pl.ds(pl.multiple_of(r * 128, 128), 128)
            total = jnp.sum(squares[rows, :] + squares_before[rows, :], axis=1, keepdims=True)
            scale = 1.0 / jnp.sqrt(total * (1.0 / width) + 1e-06)
            gate = acc[rows, :hidden] * scale
            act[rows, :] = (gate / (1.0 + jnp.exp(-gate)) * (acc[rows, hidden:] * scale)).astype(BF)

    @pl.when((step >= BLOCKS) & (step < 2 * BLOCKS))
    def _():
        out[...] = dot(act[:slots, :], w_down[...]).astype(BF)
        down[step - BLOCKS] = dot(act[slots:, :], w_down[...]).astype(BF)

    @pl.when(step == 2 * BLOCKS)
    def _():
        ungroup(down, out)


def second_half(incoming, inverse_gain, w_in, before, squares, w_down):
    slots = incoming.shape[0]
    block = inverse_gain.shape[1] // BLOCKS
    hidden, width = w_down.shape
    both = w_in.shape[-1]
    rows = before.shape[0]
    last = BLOCKS - 1
    out_block = width // BLOCKS
    return pl.pallas_call(
        second_kernel,
        grid=(2 * BLOCKS + 1,),
        in_specs=[
            columns(slots, block),
            pl.BlockSpec((slots, block), lambda i: (0, BLOCKS)),
            columns(1, block),
            weight_blocks(w_in, 1),
            pl.BlockSpec((rows // BLOCKS, both), lambda i: (jnp.minimum(i, last), 0)),
            whole((rows, 128)),
            columns(hidden, out_block, shift=BLOCKS),
        ],
        out_specs=columns(slots, out_block, shift=BLOCKS, last=BLOCKS),
        out_shape=jax.ShapeDtypeStruct((slots, width + out_block), BF),
        scratch_shapes=[
            pltpu.VMEM((rows, both), F32),
            pltpu.VMEM((rows, 128), F32),
            pltpu.VMEM((BLOCKS, rows - slots, block), BF),
            pltpu.VMEM((rows, hidden), BF),
            pltpu.VMEM((BLOCKS, rows - slots, out_block), BF),
        ],
        compiler_params=PARAMS,
        name="up_1",
    )(incoming, incoming, inverse_gain, w_in, before, squares, w_down)


def combine_kernel(
    main, extra, hidden, cot, gates_main, gates_extra, keys_main, keys_extra, out, grad, parts, dots_main, dots_extra
):
    step = pl.program_id(0)
    tokens = hidden.shape[0]

    @pl.when(step == 0)
    def _():
        regroup(extra, parts)
        dots_main[...] = jnp.zeros_like(dots_main)
        dots_extra[...] = jnp.zeros_like(dots_extra)

    rows = parts[step]
    mixed = dot(gates_main[...], main[...]) + dot(gates_extra[...], rows)
    out[...] = (hidden[...] + (mixed[:tokens] + mixed[tokens:])).astype(BF)
    dots_main[...] += lax.dot_general(cot[...], main[...], LAST, preferred_element_type=F32)
    dots_extra[...] += lax.dot_general(cot[...], rows, LAST, preferred_element_type=F32)

    @pl.when(step == BLOCKS - 1)
    def _():
        @pl.loop(0, tokens // 8)
        def _(r):
            here = pl.ds(pl.multiple_of(r * 8, 8), 8)
            of_main, of_extra = dots_main[here, :], dots_extra[here, :]
            in_main, in_extra = keys_main[here, :], keys_extra[here, :]
            main_slot = lax.broadcasted_iota(jnp.int32, of_main.shape, 1)
            extra_slot = lax.broadcasted_iota(jnp.int32, of_extra.shape, 1)
            sums = []
            for k in range(in_main.shape[1]):
                picked = jnp.where(main_slot == in_main[:, k : k + 1], of_main, 0.0)
                more = jnp.where(extra_slot == in_extra[:, k : k + 1], of_extra, 0.0)
                sums.append(jnp.sum(picked, axis=1, keepdims=True) + jnp.sum(more, axis=1, keepdims=True))
            grad[here, :] = jnp.concatenate(sums, axis=1)


def combine(returned, hidden, cot, gates_main, gates_extra, keys_main, keys_extra):
    slots = returned.shape[0]
    tokens, width = cot.shape
    block = width // BLOCKS
    extras = gates_extra.shape[1]
    top = keys_main.shape[1]
    return pl.pallas_call(
        combine_kernel,
        grid=(BLOCKS,),
        in_specs=[
            columns(slots, block),
            pl.BlockSpec((slots, block), lambda i: (0, BLOCKS)),
            columns(tokens, block),
            columns(tokens, block),
            whole(gates_main.shape),
            whole(gates_extra.shape),
            whole(keys_main.shape),
            whole(keys_extra.shape),
        ],
        out_specs=[columns(tokens, block), whole((tokens, top))],
        out_shape=[jax.ShapeDtypeStruct((tokens, width), BF), jax.ShapeDtypeStruct((tokens, top), F32)],
        scratch_shapes=[
            pltpu.VMEM((BLOCKS, extras, block), BF),
            pltpu.VMEM((tokens, slots), F32),
            pltpu.VMEM((tokens, extras), F32),
        ],
        compiler_params=PARAMS,
        name="combine",
    )(returned, returned, hidden, cot, gates_main, gates_extra, keys_main, keys_extra)


def split_in_two(values):
    high = values.astype(BF)
    return jnp.concatenate([high, (values - high.astype(F32)).astype(BF)], axis=0)


def routing(chosen, gates, experts):
    tokens = chosen.shape[0]
    hits = chosen[:, :, None] == jnp.arange(experts, dtype=jnp.int32)[None, None, :]
    member = jnp.any(hits, axis=1)
    earlier = jnp.arange(tokens)[None, :] < jnp.arange(tokens)[:, None]
    rank = dot(earlier.astype(BF), member.astype(BF)).astype(jnp.int32)
    rank = jnp.where(member, rank, -1)
    gate_of = jnp.sum(jnp.where(hits, gates[:, :, None], 0.0), axis=1)
    pair_rank = jnp.sum(jnp.where(hits, rank[:, None, :], 0), axis=2)

    def slots_of(first, count):
        return rank[:, :, None] == first + jnp.arange(count, dtype=jnp.int32)

    is_main, is_extra = slots_of(0, MAIN), slots_of(MAIN, EXTRA)
    main_hot = is_main.astype(BF).transpose(1, 2, 0).reshape(experts * MAIN, tokens)
    extra_row = jnp.arange(BLOCKS * EXTRA, dtype=jnp.int32)
    extra_rows = rank[:, :, None] == MAIN + extra_row % EXTRA
    in_block = extra_row[None, :, None, None] // EXTRA == jnp.arange(BLOCKS)[None, None, :, None]
    extra_hot = (extra_rows.transpose(1, 2, 0)[:, :, None, :] & in_block).astype(BF)
    extra_hot = extra_hot.reshape(experts * BLOCKS * EXTRA, BLOCKS * tokens)

    def gates_in(mask):
        return split_in_two(jnp.where(mask, gate_of[:, :, None], 0.0).reshape(tokens, -1))

    keys_main = jnp.where(pair_rank < MAIN, chosen * MAIN + pair_rank, -1)
    keys_extra = jnp.where(pair_rank >= MAIN, chosen * EXTRA + pair_rank - MAIN, -1)
    return main_hot, extra_hot, gates_in(is_main), gates_in(is_extra), keys_main, keys_extra


def layer(
    queries,
    rotated_keys,
    projected_values,
    doc_ids,
    residual,
    out_weight,
    norm_gain,
    routes,
    gate_vals,
    cotangent,
    expert_in,
    expert_down,
):
    seq_count = lax.axis_size("seq")
    experts = seq_count * lax.axis_size("exp")
    tokens, width = residual.shape[1:]
    shard = out_weight.shape[1]
    half = shard // CHUNKS
    by_column = out_weight.T
    weights = [
        lax.all_gather(by_column[c * half : (c + 1) * half], "exp", axis=0, tiled=True) for c in range(CHUNKS)
    ]
    in_halves = lambda a: a.reshape(a.shape[0], width // shard, CHUNKS, half)
    halves = lambda a: [in_halves(a)[:, :, c].reshape(a.shape[0], width // CHUNKS) for c in range(CHUNKS)]

    by_head = lambda a: a[0].reshape(tokens, seq_count, -1)
    heads = jnp.concatenate([by_head(queries), by_head(rotated_keys), by_head(projected_values)], axis=2)
    heads = lax.all_to_all(heads.transpose(1, 0, 2), "seq", split_axis=0, concat_axis=0, tiled=True)
    heads = heads.reshape(seq_count * tokens, -1)
    q_width = width // seq_count
    attended = attend_heads(
        heads[:, :q_width],
        heads[:, q_width : q_width + HEAD_SIZE],
        heads[:, q_width + HEAD_SIZE :],
        doc_ids[0],
    )
    place = lax.axis_index("seq").astype(jnp.int32)[None]

    def project_and_send(chunk):
        own, *sends = project(place, attended, weights[chunk], seq_count)
        arrived = []
        for shift, send in enumerate(sends, 1):
            around = [(i, (i + shift) % seq_count) for i in range(seq_count)]
            arrived.append(lax.ppermute(send, "seq", around))
        return [own, *arrived]

    def exchange(slots):
        blocks = slots.reshape(experts, MAIN, slots.shape[1])
        blocks = lax.all_to_all(blocks, ("seq", "exp"), split_axis=0, concat_axis=0, tiled=True)
        return blocks.reshape(slots.shape)

    main_hot, extra_hot, gates_main, gates_extra, keys_main, keys_extra = routing(routes[0], gate_vals[0], experts)
    residuals, gains = halves(residual[0]), halves(norm_gain[None, :])
    sums = [project_and_send(c) for c in range(CHUNKS)]
    after = [[sums[-1][0]], []]
    hidden, outgoing = zip(
        *[pack(sums[c], residuals[c], gains[c], main_hot, extra_hot, after[c]) for c in range(CHUNKS)]
    )
    incoming = [exchange(o) for o in outgoing]
    w_in = expert_in[0].reshape(width // shard, CHUNKS, half, -1)
    before, squares = first_half(incoming[0], 1.0 / gains[0], w_in)
    results = second_half(incoming[1], 1.0 / gains[1], w_in, before, squares, expert_down[0])
    hidden = jnp.stack([h.reshape(tokens, width // shard, half) for h in hidden], axis=2).reshape(tokens, width)
    layer_out, gate_grad = combine(
        exchange(results), hidden, cotangent[0], gates_main, gates_extra, keys_main, keys_extra
    )
    return layer_out[None], gate_grad[None]


def solution(mesh):
    in_specs = (
        P("exp", "seq", None),
        P("exp", "seq", None),
        P("exp", "seq", None),
        P("exp", None),
        P("exp", "seq", None),
        P("seq", "exp"),
        P(),
        P("exp", "seq", None),
        P("exp", "seq", None),
        P("exp", "seq", None),
        P(("seq", "exp"), None, None),
        P(("seq", "exp"), None, None),
    )
    out_specs = (P("exp", "seq", None), P("exp", "seq", None))
    return jax.shard_map(layer, mesh=mesh, in_specs=in_specs, out_specs=out_specs, check_vma=False)
```

```python
import math

import jax
import jax.numpy as jnp
from jax import lax
from jax.experimental import pallas as pl
from jax.experimental.pallas import tpu as pltpu
from jax.sharding import PartitionSpec as P

QUERY_HEADS = 32
KEY_VALUE_HEADS = 4
HEAD_SIZE = 128
MAIN = 8
EXTRA = 2
QUARTERS = 4
BF = jnp.bfloat16
F32 = jnp.float32
VMEM_LIMIT = 60 * 1024 * 1024
RING = 4
CORES = 2


def dot(a, b):
    return jnp.dot(a, b, preferred_element_type=F32)


def attend_heads(q_heads, k_heads, v_heads, doc_rows):
    length = q_heads.shape[0]
    group = QUERY_HEADS // KEY_VALUE_HEADS
    score_scale = 1.0 / math.sqrt(HEAD_SIZE)
    positions = jnp.arange(length)
    allowed = (positions[None, :] <= positions[:, None]) & (doc_rows[None, :] == doc_rows[:, None])
    query_block = q_heads.reshape(length, group, HEAD_SIZE)
    scores = jnp.einsum("rgd,jd->grj", query_block, k_heads, preferred_element_type=F32) * score_scale
    scores = jnp.where(allowed[None], scores, -jnp.inf)
    row_max = jnp.max(scores, axis=-1, keepdims=True)
    raised = jnp.exp(scores - row_max)
    weights_bf = (raised / jnp.sum(raised, axis=-1, keepdims=True)).astype(BF)
    block_out = jnp.einsum("grj,jd->rgd", weights_bf, v_heads, preferred_element_type=F32)
    return block_out.astype(BF).reshape(length, group * HEAD_SIZE)


def exp_shift(along_z, along_x, other_core=0):
    def place(z, x, core):
        return (z % RING * RING + x % RING) * CORES + core % CORES

    return [
        (place(z, x, core), place(z + along_z, x + along_x, core + other_core))
        for z in range(RING)
        for x in range(RING)
        for core in range(CORES)
    ]


def gather_line(part, shifts):
    return jnp.stack([part] + [lax.ppermute(part, "exp", shifts(d)) for d in range(1, RING)])


def gather_plane(line, shifts):
    gathered = [line]
    for d in range(1, RING):
        gathered.append(lax.ppermute(line, "exp", shifts(d)))
    return gathered


def project_kernel(place, mine, other, *rest):
    pieces, outs = rest[: 2 * RING], rest[2 * RING : -3]
    weight, result, arrived = rest[-3:]
    step = pl.program_id(0)
    tokens, block = outs[0].shape
    length = mine.shape[0]
    half = weight.shape[0] // 2

    @pl.when(step == 0)
    def _():
        copies = []
        for k in range(RING):
            for m in range(RING):
                for lower in range(2):
                    z, x = (m, k) if lower else (k, m)
                    chip = lax.rem(place[1] + RING - z, RING) * RING + lax.rem(place[2] + RING - x, RING)
                    lanes = pl.ds(pl.multiple_of(chip * 128, 128), 128)
                    copies.append(
                        pltpu.make_async_copy(
                            pieces[lower * RING + k].at[m],
                            weight.at[pl.ds(lower * half, half), lanes],
                            arrived.at[(k * RING + m) * 2 + lower],
                        )
                    )
        for copy in copies:
            copy.start()
        for copy in copies:
            copy.wait()

    columns = weight[:, pl.ds(pl.multiple_of(step * block, block), block)]
    result[:length, :] = dot(mine[...], columns)
    result[length:, :] = dot(other[...], columns)
    for index, out in enumerate(outs):
        pack_of, shift = divmod(index, length // tokens)
        start = pack_of * length + lax.rem(place[0] + shift, length // tokens) * tokens
        out[...] = result[pl.ds(pl.multiple_of(start, tokens), tokens), :].astype(out.dtype)


def project(place, mine, other, upper, lower, seq_count):
    length, inner = mine.shape
    tokens = length // seq_count
    width = RING * RING * 128
    steps = 4
    block = width // steps
    count = CORES * seq_count
    return pl.pallas_call(
        project_kernel,
        grid_spec=pltpu.PrefetchScalarGridSpec(
            num_scalar_prefetch=1,
            grid=(steps,),
            in_specs=[pl.BlockSpec((length, inner), lambda i, _: (0, 0))] * 2
            + [pl.BlockSpec(memory_space=pl.ANY)] * (2 * RING),
            out_specs=[pl.BlockSpec((tokens, block), lambda i, _: (0, i))] * count,
            scratch_shapes=[
                pltpu.VMEM((inner, width), BF),
                pltpu.VMEM((CORES * length, block), F32),
                pltpu.SemaphoreType.DMA((2 * RING * RING,)),
            ],
        ),
        out_shape=[jax.ShapeDtypeStruct((tokens, width), F32 if k == 0 else BF) for k in range(count)],
        compiler_params=pltpu.CompilerParams(vmem_limit_bytes=VMEM_LIMIT),
        name="project",
    )(place, mine, other, *upper, *lower)


def pack_kernel(place, *refs):
    *sums, residual, gain, main_hot, extra_hot, hidden, out, stacked = refs
    step = pl.program_id(0)
    tokens = residual.shape[0]
    quarter = stacked.shape[1]
    per_core = len(sums) // CORES

    @pl.when(step == 0)
    def _():
        total = jnp.zeros((tokens, 128), F32)
        for core in range(CORES):
            parts = sums[core * per_core : (core + 1) * per_core]
            for chip in range(RING * RING):
                value = parts[0][:, chip * 128 : (chip + 1) * 128].astype(F32)
                for part in parts[1:]:
                    value += part[:, chip * 128 : (chip + 1) * 128].astype(F32)
                shard = chip * CORES + lax.rem(place[3] + core, CORES)
                lanes = pl.ds(pl.multiple_of(shard * 128, 128), 128)
                state = residual[:, lanes].astype(F32) + value
                hidden[:, lanes] = state
                total += state * state
        mean = jnp.sum(total, axis=-1, keepdims=True) * (1.0 / hidden.shape[1])
        root_mean = jnp.sqrt(mean + 1e-06)
        for c in range(QUARTERS):
            lanes = slice(c * quarter, (c + 1) * quarter)
            stacked[c * tokens : (c + 1) * tokens, :] = (hidden[:, lanes] / root_mean * gain[:, lanes]).astype(BF)

    @pl.when(step < QUARTERS)
    def _():
        rows = stacked[pl.ds(pl.multiple_of(step * tokens, tokens), tokens), :]
        out[...] = dot(main_hot[...], rows).astype(BF)

    @pl.when(step == QUARTERS)
    def _():
        out[...] = dot(extra_hot[...], stacked[...]).astype(BF)


def pack(place, sums, residual, gain, main_hot, extra_hot):
    tokens, width = residual.shape
    quarter = width // QUARTERS
    slots = main_hot.shape[0]
    whole = lambda shape: pl.BlockSpec(shape, lambda i, _: (0, 0))
    return pl.pallas_call(
        pack_kernel,
        grid_spec=pltpu.PrefetchScalarGridSpec(
            num_scalar_prefetch=1,
            grid=(QUARTERS + 1,),
            in_specs=[whole(a.shape) for a in (*sums, residual, gain, main_hot, extra_hot)],
            out_specs=[whole((tokens, width)), pl.BlockSpec((slots, quarter), lambda i, _: (0, i))],
            scratch_shapes=[pltpu.VMEM((QUARTERS * tokens, quarter), BF)],
        ),
        out_shape=[
            jax.ShapeDtypeStruct((tokens, width), F32),
            jax.ShapeDtypeStruct((slots, width + quarter), BF),
        ],
        compiler_params=pltpu.CompilerParams(vmem_limit_bytes=VMEM_LIMIT),
        name="norm_pack",
    )(place, *sums, residual, gain, main_hot, extra_hot)


def regroup_matrix(transposed):
    size = 32 * QUARTERS * EXTRA
    grouped = lax.broadcasted_iota(jnp.int32, (size, size), 1 if transposed else 0)
    plain = lax.broadcasted_iota(jnp.int32, (size, size), 0 if transposed else 1)
    c, rest = grouped // (32 * EXTRA), grouped % (32 * EXTRA)
    source = (rest // EXTRA) * (QUARTERS * EXTRA) + c * EXTRA + rest % EXTRA
    return (source == plain).astype(F32).astype(BF)


def expert_kernel(main, extra, w_in, w_down, out, acc, act, parts):
    step = pl.program_id(0)
    slots = main.shape[0]
    hidden = act.shape[1]
    extras = parts.shape[1]
    groups = slots // 256
    per = extras // groups

    @pl.when(step == 0)
    def _():
        swap = regroup_matrix(False)
        for g in range(groups):
            rows = dot(swap, extra[g * 256 : (g + 1) * 256, :]).astype(BF)
            for c in range(QUARTERS):
                parts[c, g * per : (g + 1) * per, :] = rows[c * per : (c + 1) * per, :]

    @pl.when(step == 0)
    def _():
        acc[:slots, :] = dot(main[...], w_in[...])
        acc[slots:, :] = dot(parts[0], w_in[...])

    @pl.when((step > 0) & (step < QUARTERS))
    def _():
        acc[:slots, :] += dot(main[...], w_in[...])
        acc[slots:, :] += dot(parts[step], w_in[...])

    @pl.when(step == QUARTERS - 1)
    def _():
        gate = acc[:, :hidden]
        act[...] = (gate / (1.0 + jnp.exp(-gate)) * acc[:, hidden:]).astype(BF)

    @pl.when((step >= QUARTERS) & (step < 2 * QUARTERS))
    def _():
        out[...] = dot(act[:slots, :], w_down[...]).astype(BF)
        parts[step - QUARTERS] = dot(act[slots:, :], w_down[...]).astype(BF)

    @pl.when(step == 2 * QUARTERS)
    def _():
        swap = regroup_matrix(True)
        for g in range(groups):
            rows = jnp.concatenate([parts[c, g * per : (g + 1) * per, :] for c in range(QUARTERS)], axis=0)
            out[g * 256 : (g + 1) * 256, :] = dot(swap, rows).astype(BF)


def run_expert(incoming, w_in, w_down):
    slots = incoming.shape[0]
    width = w_in.shape[0]
    hidden = w_down.shape[0]
    quarter = width // QUARTERS
    extras = slots // MAIN * EXTRA
    last = QUARTERS - 1
    return pl.pallas_call(
        expert_kernel,
        grid=(2 * QUARTERS + 1,),
        in_specs=[
            pl.BlockSpec((slots, quarter), lambda i: (0, jnp.minimum(i, last))),
            pl.BlockSpec((slots, quarter), lambda i: (0, QUARTERS)),
            pl.BlockSpec((quarter, 2 * hidden), lambda i: (jnp.minimum(i, last), 0)),
            pl.BlockSpec((hidden, quarter), lambda i: (0, jnp.clip(i - QUARTERS, 0, last))),
        ],
        out_specs=pl.BlockSpec((slots, quarter), lambda i: (0, jnp.maximum(i - QUARTERS, 0))),
        out_shape=jax.ShapeDtypeStruct((slots, width + quarter), BF),
        scratch_shapes=[
            pltpu.VMEM((slots + extras, 2 * hidden), F32),
            pltpu.VMEM((slots + extras, hidden), BF),
            pltpu.VMEM((QUARTERS, extras, quarter), BF),
        ],
        compiler_params=pltpu.CompilerParams(vmem_limit_bytes=VMEM_LIMIT),
        name="experts",
    )(incoming, incoming, w_in, w_down)


def combine_kernel(main, extra, hidden, cot, gates_main, gates_extra, keys_main, keys_extra, out, grad, dots_main, dots_extra):
    step = pl.program_id(0)
    tokens = hidden.shape[0]
    slots = main.shape[0]
    of_quarter = lax.broadcasted_iota(jnp.int32, (1, slots), 1) % (QUARTERS * EXTRA) // EXTRA == step
    from_main = dot(gates_main[...], main[...])
    weights = jnp.where(of_quarter, gates_extra[...].astype(F32), 0.0).astype(BF)
    from_extra = dot(weights, extra[...])
    mixed = hidden[...] + (from_main[:tokens] + from_main[tokens:] + from_extra[:tokens] + from_extra[tokens:])
    out[...] = mixed.astype(BF)
    contract_last = (((1,), (1,)), ((), ()))
    new_main = lax.dot_general(cot[...], main[...], contract_last, preferred_element_type=F32)
    new_extra = lax.dot_general(cot[...], extra[...], contract_last, preferred_element_type=F32)
    new_extra = jnp.where(of_quarter, new_extra, 0.0)

    @pl.when(step == 0)
    def _():
        dots_main[...] = new_main
        dots_extra[...] = new_extra

    @pl.when(step > 0)
    def _():
        dots_main[...] += new_main
        dots_extra[...] += new_extra

    @pl.when(step == QUARTERS - 1)
    def _():
        slot = lax.broadcasted_iota(jnp.int32, (tokens, slots), 1)
        extra_slot = slot // (QUARTERS * EXTRA) * EXTRA + slot % EXTRA
        sums = []
        for k in range(keys_main.shape[1]):
            picked = jnp.where(slot == keys_main[:, k : k + 1], dots_main[...], 0.0)
            picked += jnp.where(extra_slot == keys_extra[:, k : k + 1], dots_extra[...], 0.0)
            sums.append(jnp.sum(picked, axis=1, keepdims=True))
        grad[...] = jnp.concatenate(sums, axis=1)


def combine(returned, hidden, cot, gates_main, gates_extra, keys_main, keys_extra):
    slots = returned.shape[0]
    tokens, width = hidden.shape
    quarter = width // QUARTERS
    top = keys_main.shape[1]
    whole = lambda shape: pl.BlockSpec(shape, lambda i: (0, 0))
    part = lambda shape: pl.BlockSpec(shape, lambda i: (0, i))
    return pl.pallas_call(
        combine_kernel,
        grid=(QUARTERS,),
        in_specs=[
            part((slots, quarter)),
            pl.BlockSpec((slots, quarter), lambda i: (0, QUARTERS)),
            part((tokens, quarter)),
            part((tokens, quarter)),
            whole(gates_main.shape),
            whole(gates_extra.shape),
            whole(keys_main.shape),
            whole(keys_extra.shape),
        ],
        out_specs=[part((tokens, quarter)), whole((tokens, top))],
        out_shape=[jax.ShapeDtypeStruct((tokens, width), BF), jax.ShapeDtypeStruct((tokens, top), F32)],
        scratch_shapes=[pltpu.VMEM((tokens, slots), F32), pltpu.VMEM((tokens, slots), F32)],
        compiler_params=pltpu.CompilerParams(vmem_limit_bytes=VMEM_LIMIT),
        name="combine",
    )(returned, returned, hidden, cot, gates_main, gates_extra, keys_main, keys_extra)


def split_in_two(values):
    high = values.astype(BF)
    return jnp.concatenate([high, (values - high.astype(F32)).astype(BF)], axis=0)


def routing(chosen, gates, experts):
    tokens = chosen.shape[0]
    hits = chosen[:, :, None] == jnp.arange(experts, dtype=jnp.int32)[None, None, :]
    member = jnp.any(hits, axis=1)
    earlier = jnp.arange(tokens)[None, :] < jnp.arange(tokens)[:, None]
    rank = dot(earlier.astype(BF), member.astype(BF)).astype(jnp.int32)
    rank = jnp.where(member, rank, -1)
    gate_of = jnp.sum(jnp.where(hits, gates[:, :, None], 0.0), axis=1)
    pair_rank = jnp.sum(jnp.where(hits, rank[:, None, :], 0), axis=2)

    is_main = rank[:, :, None] == jnp.arange(MAIN, dtype=jnp.int32)
    extra_row = jnp.arange(QUARTERS * EXTRA, dtype=jnp.int32)
    is_extra = rank[:, :, None] == MAIN + extra_row % EXTRA
    main_hot = is_main.astype(BF).transpose(1, 2, 0).reshape(experts * MAIN, tokens)
    in_quarter = extra_row[None, :, None, None] // EXTRA == jnp.arange(QUARTERS)[None, None, :, None]
    extra_hot = (is_extra.transpose(1, 2, 0)[:, :, None, :] & in_quarter).astype(BF)
    extra_hot = extra_hot.reshape(experts * QUARTERS * EXTRA, QUARTERS * tokens)

    gates_main = jnp.where(is_main, gate_of[:, :, None], 0.0).reshape(tokens, experts * MAIN)
    gates_extra = jnp.where(is_extra, gate_of[:, :, None], 0.0).reshape(tokens, experts * QUARTERS * EXTRA)
    keys_main = jnp.where(pair_rank < MAIN, chosen * MAIN + pair_rank, -1)
    keys_extra = jnp.where(pair_rank >= MAIN, chosen * EXTRA + pair_rank - MAIN, -1)
    return main_hot, extra_hot, split_in_two(gates_main), split_in_two(gates_extra), keys_main, keys_extra


def layer(
    queries,
    rotated_keys,
    projected_values,
    doc_ids,
    residual,
    out_weight,
    norm_gain,
    routes,
    gate_vals,
    cotangent,
    expert_in,
    expert_down,
):
    seq_count = lax.axis_size("seq")
    experts = seq_count * lax.axis_size("exp")
    tokens, width = residual.shape[1:]
    along_x, along_z = lambda d: exp_shift(0, d), lambda d: exp_shift(d, 0)
    half = out_weight.shape[0] // 2
    upper = gather_line(out_weight[:half], along_x)
    lower = gather_line(out_weight[half:], along_z)

    by_head = lambda a: a[0].reshape(tokens, seq_count, -1)
    heads = jnp.concatenate([by_head(queries), by_head(rotated_keys), by_head(projected_values)], axis=2)
    heads = lax.all_to_all(heads.transpose(1, 0, 2), "seq", split_axis=0, concat_axis=0, tiled=True)
    heads, upper, lower = lax.optimization_barrier((heads, upper, lower))
    upper, lower = gather_plane(upper, along_z), gather_plane(lower, along_x)
    heads = heads.reshape(seq_count * tokens, -1)
    q_width = width // seq_count
    attended = attend_heads(
        heads[:, :q_width],
        heads[:, q_width : q_width + HEAD_SIZE],
        heads[:, q_width + HEAD_SIZE :],
        doc_ids[0],
    )
    other = lax.ppermute(attended, "exp", exp_shift(0, 0, 1))
    seq, exp = lax.axis_index("seq"), lax.axis_index("exp")
    place = jnp.stack([seq, exp // (RING * CORES), exp // CORES % RING, exp % CORES]).astype(jnp.int32)
    sums = list(project(place, attended, other, upper, lower, seq_count))
    for index in range(1, len(sums)):
        core, shift = divmod(index, seq_count)
        around = [
            (s * RING * RING * CORES + a, (s + shift) % seq_count * RING * RING * CORES + b)
            for s in range(seq_count)
            for a, b in exp_shift(0, 0, core)
        ]
        sums[index] = lax.ppermute(sums[index], ("seq", "exp"), around)

    main_hot, extra_hot, gates_main, gates_extra, keys_main, keys_extra = routing(routes[0], gate_vals[0], experts)
    hidden, outgoing = pack(place, sums, residual[0], norm_gain[None, :], main_hot, extra_hot)

    def exchange(slots):
        blocks = slots.reshape(experts, MAIN, slots.shape[1])
        blocks = lax.all_to_all(blocks, ("seq", "exp"), split_axis=0, concat_axis=0, tiled=True)
        return blocks.reshape(slots.shape)

    results = run_expert(exchange(outgoing), expert_in[0], expert_down[0])
    layer_out, gate_grad = combine(
        exchange(results), hidden, cotangent[0], gates_main, gates_extra, keys_main, keys_extra
    )
    return layer_out[None], gate_grad[None]


def solution(mesh):
    in_specs = (
        P("exp", "seq", None),
        P("exp", "seq", None),
        P("exp", "seq", None),
        P("exp", None),
        P("exp", "seq", None),
        P("seq", "exp"),
        P(),
        P("exp", "seq", None),
        P("exp", "seq", None),
        P("exp", "seq", None),
        P(("seq", "exp"), None, None),
        P(("seq", "exp"), None, None),
    )
    out_specs = (P("exp", "seq", None), P("exp", "seq", None))
    return jax.shard_map(layer, mesh=mesh, in_specs=in_specs, out_specs=out_specs, check_vma=False)
```

```python
import math

import jax
import jax.numpy as jnp
from jax import lax
from jax.experimental import pallas as pl
from jax.experimental.pallas import tpu as pltpu
from jax.sharding import PartitionSpec as P

QUERY_HEADS = 32
KEY_VALUE_HEADS = 4
HEAD_SIZE = 128
MAIN = 8
EXTRA = 2
QUARTERS = 4
BF = jnp.bfloat16
F32 = jnp.float32
VMEM_LIMIT = 60 * 1024 * 1024
RING = 4
CORES = 2


def dot(a, b):
    return jnp.dot(a, b, preferred_element_type=F32)


def attend_heads(q_heads, k_heads, v_heads, doc_rows):
    length = q_heads.shape[0]
    group = QUERY_HEADS // KEY_VALUE_HEADS
    score_scale = 1.0 / math.sqrt(HEAD_SIZE)
    positions = jnp.arange(length)
    allowed = (positions[None, :] <= positions[:, None]) & (doc_rows[None, :] == doc_rows[:, None])
    query_block = q_heads.reshape(length, group, HEAD_SIZE)
    scores = jnp.einsum("rgd,jd->grj", query_block, k_heads, preferred_element_type=F32) * score_scale
    scores = jnp.where(allowed[None], scores, -jnp.inf)
    row_max = jnp.max(scores, axis=-1, keepdims=True)
    raised = jnp.exp(scores - row_max)
    weights_bf = (raised / jnp.sum(raised, axis=-1, keepdims=True)).astype(BF)
    block_out = jnp.einsum("grj,jd->rgd", weights_bf, v_heads, preferred_element_type=F32)
    return block_out.astype(BF).reshape(length, group * HEAD_SIZE)


def exp_shift(along_z, along_x, other_core=0):
    def place(z, x, core):
        return (z % RING * RING + x % RING) * CORES + core % CORES

    return [
        (place(z, x, core), place(z + along_z, x + along_x, core + other_core))
        for z in range(RING)
        for x in range(RING)
        for core in range(CORES)
    ]


def gather_line(part, shifts):
    return jnp.stack([part] + [lax.ppermute(part, "exp", shifts(d)) for d in range(1, RING)])


def gather_plane(line, shifts):
    gathered = [line]
    for d in range(1, RING):
        gathered.append(lax.ppermute(line, "exp", shifts(d)))
    return gathered


def project_kernel(place, mine, other, *rest):
    pieces, outs = rest[: 2 * RING], rest[2 * RING : -3]
    weight, result, arrived = rest[-3:]
    step = pl.program_id(0)
    tokens, block = outs[0].shape
    length = mine.shape[0]
    half = weight.shape[0] // 2

    @pl.when(step == 0)
    def _():
        copies = []
        for k in range(RING):
            for m in range(RING):
                for lower in range(2):
                    z, x = (m, k) if lower else (k, m)
                    chip = lax.rem(place[1] + RING - z, RING) * RING + lax.rem(place[2] + RING - x, RING)
                    lanes = pl.ds(pl.multiple_of(chip * 128, 128), 128)
                    copies.append(
                        pltpu.make_async_copy(
                            pieces[lower * RING + k].at[m],
                            weight.at[pl.ds(lower * half, half), lanes],
                            arrived.at[(k * RING + m) * 2 + lower],
                        )
                    )
        for copy in copies:
            copy.start()
        for copy in copies:
            copy.wait()

    columns = weight[:, pl.ds(pl.multiple_of(step * block, block), block)]
    result[:length, :] = dot(mine[...], columns)
    result[length:, :] = dot(other[...], columns)
    for index, out in enumerate(outs):
        pack_of, shift = divmod(index, length // tokens)
        start = pack_of * length + lax.rem(place[0] + shift, length // tokens) * tokens
        out[...] = result[pl.ds(pl.multiple_of(start, tokens), tokens), :].astype(out.dtype)


def project(place, mine, other, upper, lower, seq_count):
    length, inner = mine.shape
    tokens = length // seq_count
    width = RING * RING * 128
    steps = 4
    block = width // steps
    count = CORES * seq_count
    return pl.pallas_call(
        project_kernel,
        grid_spec=pltpu.PrefetchScalarGridSpec(
            num_scalar_prefetch=1,
            grid=(steps,),
            in_specs=[pl.BlockSpec((length, inner), lambda i, _: (0, 0))] * 2
            + [pl.BlockSpec(memory_space=pl.ANY)] * (2 * RING),
            out_specs=[pl.BlockSpec((tokens, block), lambda i, _: (0, i))] * count,
            scratch_shapes=[
                pltpu.VMEM((inner, width), BF),
                pltpu.VMEM((CORES * length, block), F32),
                pltpu.SemaphoreType.DMA((2 * RING * RING,)),
            ],
        ),
        out_shape=[jax.ShapeDtypeStruct((tokens, width), F32 if k == 0 else BF) for k in range(count)],
        compiler_params=pltpu.CompilerParams(vmem_limit_bytes=VMEM_LIMIT),
        name="project",
    )(place, mine, other, *upper, *lower)


def pack_kernel(place, *refs):
    *sums, residual, gain, main_hot, extra_hot, hidden, out, stacked = refs
    step = pl.program_id(0)
    tokens = residual.shape[0]
    quarter = stacked.shape[1]
    per_core = len(sums) // CORES

    @pl.when(step == 0)
    def _():
        total = jnp.zeros((tokens, 128), F32)
        for core in range(CORES):
            parts = sums[core * per_core : (core + 1) * per_core]
            for chip in range(RING * RING):
                value = parts[0][:, chip * 128 : (chip + 1) * 128].astype(F32)
                for part in parts[1:]:
                    value += part[:, chip * 128 : (chip + 1) * 128].astype(F32)
                shard = chip * CORES + lax.rem(place[3] + core, CORES)
                lanes = pl.ds(pl.multiple_of(shard * 128, 128), 128)
                state = residual[:, lanes].astype(F32) + value
                hidden[:, lanes] = state
                total += state * state
        mean = jnp.sum(total, axis=-1, keepdims=True) * (1.0 / hidden.shape[1])
        scale = 1.0 / jnp.sqrt(mean + 1e-06)
        for c in range(QUARTERS):
            lanes = slice(c * quarter, (c + 1) * quarter)
            stacked[c * tokens : (c + 1) * tokens, :] = (hidden[:, lanes] * scale * gain[:, lanes]).astype(BF)

    @pl.when(step < QUARTERS)
    def _():
        rows = stacked[pl.ds(pl.multiple_of(step * tokens, tokens), tokens), :]
        out[...] = dot(main_hot[...], rows).astype(BF)

    @pl.when(step == QUARTERS)
    def _():
        out[...] = dot(extra_hot[...], stacked[...]).astype(BF)


def pack(place, sums, residual, gain, main_hot, extra_hot):
    tokens, width = residual.shape
    quarter = width // QUARTERS
    slots = main_hot.shape[0]
    whole = lambda shape: pl.BlockSpec(shape, lambda i, _: (0, 0))
    return pl.pallas_call(
        pack_kernel,
        grid_spec=pltpu.PrefetchScalarGridSpec(
            num_scalar_prefetch=1,
            grid=(QUARTERS + 1,),
            in_specs=[whole(a.shape) for a in (*sums, residual, gain, main_hot, extra_hot)],
            out_specs=[whole((tokens, width)), pl.BlockSpec((slots, quarter), lambda i, _: (0, i))],
            scratch_shapes=[pltpu.VMEM((QUARTERS * tokens, quarter), BF)],
        ),
        out_shape=[
            jax.ShapeDtypeStruct((tokens, width), F32),
            jax.ShapeDtypeStruct((slots, width + quarter), BF),
        ],
        compiler_params=pltpu.CompilerParams(vmem_limit_bytes=VMEM_LIMIT),
        name="norm_pack",
    )(place, *sums, residual, gain, main_hot, extra_hot)


def regroup_matrix(transposed):
    size = 32 * QUARTERS * EXTRA
    grouped = lax.broadcasted_iota(jnp.int32, (size, size), 1 if transposed else 0)
    plain = lax.broadcasted_iota(jnp.int32, (size, size), 0 if transposed else 1)
    c, rest = grouped // (32 * EXTRA), grouped % (32 * EXTRA)
    source = (rest // EXTRA) * (QUARTERS * EXTRA) + c * EXTRA + rest % EXTRA
    return (source == plain).astype(F32).astype(BF)


def regroup(extra, parts):
    size = 32 * QUARTERS * EXTRA
    per = 32 * EXTRA
    swap = regroup_matrix(False)
    for g in range(extra.shape[0] // size):
        rows = dot(swap, extra[g * size : (g + 1) * size, :]).astype(BF)
        for c in range(QUARTERS):
            parts[c, g * per : (g + 1) * per, :] = rows[c * per : (c + 1) * per, :]


def ungroup(parts, out):
    size = 32 * QUARTERS * EXTRA
    per = 32 * EXTRA
    swap = regroup_matrix(True)
    for g in range(out.shape[0] // size):
        rows = jnp.concatenate([parts[c, g * per : (g + 1) * per, :] for c in range(QUARTERS)], axis=0)
        out[g * size : (g + 1) * size, :] = dot(swap, rows).astype(BF)


def up_step(step, rows, w_in, acc, act):
    hidden = act.shape[1]

    @pl.when(step == 0)
    def _():
        @pl.loop(0, acc.shape[0] // 64)
        def _(r):
            acc[pl.ds(pl.multiple_of(r * 64, 64), 64), :] = jnp.zeros((64, acc.shape[1]), F32)

    acc[...] += dot(rows, w_in[...])

    @pl.when(step == QUARTERS - 1)
    def _():
        gate = acc[:, :hidden]
        act[...] = (gate / (1.0 + jnp.exp(-gate)) * acc[:, hidden:]).astype(BF)


def main_kernel(after, main, w_in, w_down, out, acc, act):
    step = pl.program_id(0)

    @pl.when(step < QUARTERS)
    def _():
        up_step(step, main[...], w_in, acc, act)

    @pl.when(step >= QUARTERS)
    def _():
        out[...] = dot(act[...], w_down[...]).astype(BF)


def extra_kernel(extra, w_in, w_down, out, acc, act, parts):
    step = pl.program_id(0)

    @pl.when(step == 0)
    def _():
        regroup(extra, parts)

    @pl.when(step < QUARTERS)
    def _():
        up_step(step, parts[step], w_in, acc, act)

    @pl.when(step >= QUARTERS)
    def _():
        parts[step - QUARTERS] = dot(act[...], w_down[...]).astype(BF)

    @pl.when(step == 2 * QUARTERS - 1)
    def _():
        ungroup(parts, out)


def run_expert(incoming, w_in, w_down, after=None):
    slots = incoming.shape[0]
    width = w_in.shape[0]
    hidden = w_down.shape[0]
    quarter = width // QUARTERS
    last = QUARTERS - 1
    main = after is not None
    rows = slots if main else slots // MAIN * EXTRA
    if main:
        in_specs = [
            pl.BlockSpec(memory_space=pl.ANY),
            pl.BlockSpec((slots, quarter), lambda i: (0, jnp.minimum(i, last))),
        ]
        out_specs = pl.BlockSpec((slots, quarter), lambda i: (0, jnp.maximum(i - QUARTERS, 0)))
        out_width, scratch = width, []
    else:
        in_specs = [pl.BlockSpec((slots, quarter), lambda i: (0, QUARTERS))]
        out_specs = pl.BlockSpec((slots, quarter), lambda i: (0, 0))
        out_width, scratch = quarter, [pltpu.VMEM((QUARTERS, rows, quarter), BF)]
    return pl.pallas_call(
        main_kernel if main else extra_kernel,
        grid=(2 * QUARTERS,),
        in_specs=in_specs
        + [
            pl.BlockSpec((quarter, 2 * hidden), lambda i: (jnp.minimum(i, last), 0)),
            pl.BlockSpec((hidden, quarter), lambda i: (0, jnp.clip(i - QUARTERS, 0, last))),
        ],
        out_specs=out_specs,
        out_shape=jax.ShapeDtypeStruct((slots, out_width), BF),
        scratch_shapes=[pltpu.VMEM((rows, 2 * hidden), F32), pltpu.VMEM((rows, hidden), BF)] + scratch,
        compiler_params=pltpu.CompilerParams(vmem_limit_bytes=VMEM_LIMIT),
        name="experts_main" if main else "experts_extra",
    )(*([after] if main else []), incoming, w_in, w_down)


def select_dots(dots, keys):
    slot = lax.broadcasted_iota(jnp.int32, dots.shape, 1)
    column = lax.broadcasted_iota(jnp.int32, (dots.shape[0], 128), 1)
    picked = jnp.zeros((dots.shape[0], 128), F32)
    for k in range(keys.shape[1]):
        entry = jnp.sum(jnp.where(slot == keys[:, k : k + 1], dots[...], 0.0), axis=1, keepdims=True)
        picked = jnp.where(column == k, entry, picked)
    return picked


def combine_step(rows, hidden, cot, gates, out, dots):
    step = pl.program_id(0)
    tokens = hidden.shape[0]
    mixed = dot(gates[...], rows)
    out[...] = (hidden[...] + (mixed[:tokens] + mixed[tokens:])).astype(out.dtype)
    more = lax.dot_general(cot[...], rows, (((1,), (1,)), ((), ())), preferred_element_type=F32)

    @pl.when(step == 0)
    def _():
        dots[...] = more

    @pl.when(step > 0)
    def _():
        dots[...] += more


def combine_extra(extra, hidden, cot, gates, keys, out, grad, dots, parts):
    step = pl.program_id(0)

    @pl.when(step == 0)
    def _():
        regroup(extra, parts)

    combine_step(parts[step], hidden, cot, gates, out, dots)

    @pl.when(step == QUARTERS - 1)
    def _():
        grad[...] = select_dots(dots, keys)


def combine_main(main, hidden, cot, gates, keys, before, out, grad, dots):
    combine_step(main[...], hidden, cot, gates, out, dots)

    @pl.when(pl.program_id(0) == QUARTERS - 1)
    def _():
        grad[...] = (select_dots(dots, keys) + before[...]).T[: keys.shape[1], :]


def combine(returned, hidden, cot, gates, keys, before=None):
    slots = returned.shape[0]
    tokens, width = hidden.shape
    quarter = width // QUARTERS
    top = keys.shape[1]
    count = gates.shape[1]
    whole = lambda shape: pl.BlockSpec(shape, lambda i: (0, 0))
    part = lambda shape: pl.BlockSpec(shape, lambda i: (0, i))
    main = before is not None
    more = [before] if main else []
    grad = (top, tokens) if main else (tokens, 128)
    return pl.pallas_call(
        combine_main if main else combine_extra,
        grid=(QUARTERS,),
        in_specs=[
            part((slots, quarter)) if main else whole((slots, quarter)),
            part((tokens, quarter)),
            part((tokens, quarter)),
        ]
        + [whole(a.shape) for a in (gates, keys, *more)],
        out_specs=[part((tokens, quarter)), whole(grad)],
        out_shape=[
            jax.ShapeDtypeStruct((tokens, width), BF if main else F32),
            jax.ShapeDtypeStruct(grad, F32),
        ],
        scratch_shapes=[pltpu.VMEM((tokens, count), F32)]
        + ([] if main else [pltpu.VMEM((QUARTERS, count, quarter), BF)]),
        compiler_params=pltpu.CompilerParams(vmem_limit_bytes=VMEM_LIMIT),
        name="combine_main" if main else "combine_extra",
    )(returned, hidden, cot, gates, keys, *more)


def split_in_two(values):
    high = values.astype(BF)
    return jnp.concatenate([high, (values - high.astype(F32)).astype(BF)], axis=0)


def routing(chosen, gates, experts):
    tokens = chosen.shape[0]
    hits = chosen[:, :, None] == jnp.arange(experts, dtype=jnp.int32)[None, None, :]
    member = jnp.any(hits, axis=1)
    earlier = jnp.arange(tokens)[None, :] < jnp.arange(tokens)[:, None]
    rank = dot(earlier.astype(BF), member.astype(BF)).astype(jnp.int32)
    rank = jnp.where(member, rank, -1)
    gate_of = jnp.sum(jnp.where(hits, gates[:, :, None], 0.0), axis=1)
    pair_rank = jnp.sum(jnp.where(hits, rank[:, None, :], 0), axis=2)

    is_main = rank[:, :, None] == jnp.arange(MAIN, dtype=jnp.int32)
    extra_row = jnp.arange(QUARTERS * EXTRA, dtype=jnp.int32)
    is_extra = rank[:, :, None] == MAIN + extra_row % EXTRA
    main_hot = is_main.astype(BF).transpose(1, 2, 0).reshape(experts * MAIN, tokens)
    in_quarter = extra_row[None, :, None, None] // EXTRA == jnp.arange(QUARTERS)[None, None, :, None]
    extra_hot = (is_extra.transpose(1, 2, 0)[:, :, None, :] & in_quarter).astype(BF)
    extra_hot = extra_hot.reshape(experts * QUARTERS * EXTRA, QUARTERS * tokens)

    gates_main = jnp.where(is_main, gate_of[:, :, None], 0.0).reshape(tokens, experts * MAIN)
    is_extra = rank[:, :, None] == MAIN + jnp.arange(EXTRA, dtype=jnp.int32)
    gates_extra = jnp.where(is_extra, gate_of[:, :, None], 0.0).reshape(tokens, experts * EXTRA)
    keys_main = jnp.where(pair_rank < MAIN, chosen * MAIN + pair_rank, -1)
    keys_extra = jnp.where(pair_rank >= MAIN, chosen * EXTRA + pair_rank - MAIN, -1)
    return main_hot, extra_hot, split_in_two(gates_main), split_in_two(gates_extra), keys_main, keys_extra


def layer(
    queries,
    rotated_keys,
    projected_values,
    doc_ids,
    residual,
    out_weight,
    norm_gain,
    routes,
    gate_vals,
    cotangent,
    expert_in,
    expert_down,
):
    seq_count = lax.axis_size("seq")
    experts = seq_count * lax.axis_size("exp")
    tokens, width = residual.shape[1:]
    along_x, along_z = lambda d: exp_shift(0, d), lambda d: exp_shift(d, 0)
    half = out_weight.shape[0] // 2
    upper = gather_line(out_weight[:half], along_x)
    lower = gather_line(out_weight[half:], along_z)

    by_head = lambda a: a[0].reshape(tokens, seq_count, -1)
    heads = jnp.concatenate([by_head(queries), by_head(rotated_keys), by_head(projected_values)], axis=2)
    heads = lax.all_to_all(heads.transpose(1, 0, 2), "seq", split_axis=0, concat_axis=0, tiled=True)
    heads, upper, lower = lax.optimization_barrier((heads, upper, lower))
    upper, lower = gather_plane(upper, along_z), gather_plane(lower, along_x)
    heads = heads.reshape(seq_count * tokens, -1)
    q_width = width // seq_count
    attended = attend_heads(
        heads[:, :q_width],
        heads[:, q_width : q_width + HEAD_SIZE],
        heads[:, q_width + HEAD_SIZE :],
        doc_ids[0],
    )
    other = lax.ppermute(attended, "exp", exp_shift(0, 0, 1))
    seq, exp = lax.axis_index("seq"), lax.axis_index("exp")
    place = jnp.stack([seq, exp // (RING * CORES), exp // CORES % RING, exp % CORES]).astype(jnp.int32)
    sums = list(project(place, attended, other, upper, lower, seq_count))
    for index in range(1, len(sums)):
        core, shift = divmod(index, seq_count)
        around = [
            (s * RING * RING * CORES + a, (s + shift) % seq_count * RING * RING * CORES + b)
            for s in range(seq_count)
            for a, b in exp_shift(0, 0, core)
        ]
        sums[index] = lax.ppermute(sums[index], ("seq", "exp"), around)

    main_hot, extra_hot, gates_main, gates_extra, keys_main, keys_extra = routing(routes[0], gate_vals[0], experts)
    hidden, outgoing = pack(place, sums, residual[0], norm_gain[None, :], main_hot, extra_hot)

    def exchange(slots):
        blocks = slots.reshape(experts, MAIN, slots.shape[1])
        blocks = lax.all_to_all(blocks, ("seq", "exp"), split_axis=0, concat_axis=0, tiled=True)
        return blocks.reshape(slots.shape)

    incoming = exchange(outgoing)
    results = run_expert(incoming, expert_in[0], expert_down[0])
    returned = exchange(results)
    main_results = run_expert(incoming, expert_in[0], expert_down[0], after=results)
    cot = cotangent[0]
    hidden, grad = combine(returned, hidden, cot, gates_extra, keys_extra)
    returned = exchange(main_results)
    layer_out, gate_grad = combine(returned, hidden, cot, gates_main, keys_main, grad)
    return layer_out[None], gate_grad.T[None]


def solution(mesh):
    in_specs = (
        P("exp", "seq", None),
        P("exp", "seq", None),
        P("exp", "seq", None),
        P("exp", None),
        P("exp", "seq", None),
        P("seq", "exp"),
        P(),
        P("exp", "seq", None),
        P("exp", "seq", None),
        P("exp", "seq", None),
        P(("seq", "exp"), None, None),
        P(("seq", "exp"), None, None),
    )
    out_specs = (P("exp", "seq", None), P("exp", "seq", None))
    return jax.shard_map(layer, mesh=mesh, in_specs=in_specs, out_specs=out_specs, check_vma=False)
```

```python
import math

import jax
import jax.numpy as jnp
from jax import lax
from jax.experimental import pallas as pl
from jax.experimental.pallas import tpu as pltpu
from jax.sharding import PartitionSpec as P

QUERY_HEADS = 32
KEY_VALUE_HEADS = 4
HEAD_SIZE = 128
MAIN = 8
EXTRA = 2
QUARTERS = 4
BF = jnp.bfloat16
F32 = jnp.float32
VMEM_LIMIT = 60 * 1024 * 1024
RING = 4
CORES = 2


def dot(a, b):
    return jnp.dot(a, b, preferred_element_type=F32)


def attend_heads(q_heads, k_heads, v_heads, doc_rows):
    length = q_heads.shape[0]
    group = QUERY_HEADS // KEY_VALUE_HEADS
    score_scale = 1.0 / math.sqrt(HEAD_SIZE)
    positions = jnp.arange(length)
    allowed = (positions[None, :] <= positions[:, None]) & (doc_rows[None, :] == doc_rows[:, None])
    query_block = q_heads.reshape(length, group, HEAD_SIZE)
    scores = jnp.einsum("rgd,jd->grj", query_block, k_heads, preferred_element_type=F32) * score_scale
    scores = jnp.where(allowed[None], scores, -jnp.inf)
    row_max = jnp.max(scores, axis=-1, keepdims=True)
    raised = jnp.exp(scores - row_max)
    weights_bf = (raised / jnp.sum(raised, axis=-1, keepdims=True)).astype(BF)
    block_out = jnp.einsum("grj,jd->rgd", weights_bf, v_heads, preferred_element_type=F32)
    return block_out.astype(BF).reshape(length, group * HEAD_SIZE)


def exp_shift(along_z, along_x, other_core=0):
    def place(z, x, core):
        return (z % RING * RING + x % RING) * CORES + core % CORES

    return [
        (place(z, x, core), place(z + along_z, x + along_x, core + other_core))
        for z in range(RING)
        for x in range(RING)
        for core in range(CORES)
    ]


def gather_line(part, shifts):
    return jnp.stack([part] + [lax.ppermute(part, "exp", shifts(d)) for d in range(1, RING)])


def gather_plane(line, shifts):
    gathered = [line]
    for d in range(1, RING):
        gathered.append(lax.ppermute(line, "exp", shifts(d)))
    return gathered


def project_kernel(place, mine, other, *rest):
    pieces, outs = rest[: 2 * RING], rest[2 * RING : -3]
    weight, result, arrived = rest[-3:]
    step = pl.program_id(0)
    tokens, block = outs[0].shape
    length = mine.shape[0]
    half = weight.shape[0] // 2

    @pl.when(step == 0)
    def _():
        copies = []
        for k in range(RING):
            for m in range(RING):
                for lower in range(2):
                    z, x = (m, k) if lower else (k, m)
                    chip = lax.rem(place[1] + RING - z, RING) * RING + lax.rem(place[2] + RING - x, RING)
                    lanes = pl.ds(pl.multiple_of(chip * 128, 128), 128)
                    copies.append(
                        pltpu.make_async_copy(
                            pieces[lower * RING + k].at[m],
                            weight.at[pl.ds(lower * half, half), lanes],
                            arrived.at[(k * RING + m) * 2 + lower],
                        )
                    )
        for copy in copies:
            copy.start()
        for copy in copies:
            copy.wait()

    columns = weight[:, pl.ds(pl.multiple_of(step * block, block), block)]
    result[:length, :] = dot(mine[...], columns)
    result[length:, :] = dot(other[...], columns)
    for index, out in enumerate(outs):
        pack_of, shift = divmod(index, length // tokens)
        start = pack_of * length + lax.rem(place[0] + shift, length // tokens) * tokens
        out[...] = result[pl.ds(pl.multiple_of(start, tokens), tokens), :].astype(out.dtype)


def project(place, mine, other, upper, lower, seq_count):
    length, inner = mine.shape
    tokens = length // seq_count
    width = RING * RING * 128
    steps = 4
    block = width // steps
    count = CORES * seq_count
    return pl.pallas_call(
        project_kernel,
        grid_spec=pltpu.PrefetchScalarGridSpec(
            num_scalar_prefetch=1,
            grid=(steps,),
            in_specs=[pl.BlockSpec((length, inner), lambda i, _: (0, 0))] * 2
            + [pl.BlockSpec(memory_space=pl.ANY)] * (2 * RING),
            out_specs=[pl.BlockSpec((tokens, block), lambda i, _: (0, i))] * count,
            scratch_shapes=[
                pltpu.VMEM((inner, width), BF),
                pltpu.VMEM((CORES * length, block), F32),
                pltpu.SemaphoreType.DMA((2 * RING * RING,)),
            ],
        ),
        out_shape=[jax.ShapeDtypeStruct((tokens, width), F32 if k == 0 else BF) for k in range(count)],
        compiler_params=pltpu.CompilerParams(vmem_limit_bytes=VMEM_LIMIT),
        name="project",
    )(place, mine, other, *upper, *lower)


def pack_kernel(place, *refs):
    *sums, residual, gain, main_hot, extra_hot, hidden, out, stacked = refs
    step = pl.program_id(0)
    tokens = residual.shape[0]
    quarter = stacked.shape[1]
    per_core = len(sums) // CORES

    @pl.when(step == 0)
    def _():
        total = jnp.zeros((tokens, 128), F32)
        for core in range(CORES):
            parts = sums[core * per_core : (core + 1) * per_core]
            for chip in range(RING * RING):
                value = parts[0][:, chip * 128 : (chip + 1) * 128].astype(F32)
                for part in parts[1:]:
                    value += part[:, chip * 128 : (chip + 1) * 128].astype(F32)
                shard = chip * CORES + lax.rem(place[3] + core, CORES)
                lanes = pl.ds(pl.multiple_of(shard * 128, 128), 128)
                state = residual[:, lanes].astype(F32) + value
                hidden[:, lanes] = state
                total += state * state
        mean = jnp.sum(total, axis=-1, keepdims=True) * (1.0 / hidden.shape[1])
        scale = 1.0 / jnp.sqrt(mean + 1e-06)
        for c in range(QUARTERS):
            lanes = slice(c * quarter, (c + 1) * quarter)
            stacked[c * tokens : (c + 1) * tokens, :] = (hidden[:, lanes] * scale * gain[:, lanes]).astype(BF)

    @pl.when(step < QUARTERS)
    def _():
        rows = stacked[pl.ds(pl.multiple_of(step * tokens, tokens), tokens), :]
        out[...] = dot(main_hot[...], rows).astype(BF)

    @pl.when(step == QUARTERS)
    def _():
        out[...] = dot(extra_hot[...], stacked[...]).astype(BF)


def pack(place, sums, residual, gain, main_hot, extra_hot):
    tokens, width = residual.shape
    quarter = width // QUARTERS
    slots = main_hot.shape[0]
    whole = lambda shape: pl.BlockSpec(shape, lambda i, _: (0, 0))
    return pl.pallas_call(
        pack_kernel,
        grid_spec=pltpu.PrefetchScalarGridSpec(
            num_scalar_prefetch=1,
            grid=(QUARTERS + 1,),
            in_specs=[whole(a.shape) for a in (*sums, residual, gain, main_hot, extra_hot)],
            out_specs=[whole((tokens, width)), pl.BlockSpec((slots, quarter), lambda i, _: (0, i))],
            scratch_shapes=[pltpu.VMEM((QUARTERS * tokens, quarter), BF)],
        ),
        out_shape=[
            jax.ShapeDtypeStruct((tokens, width), F32),
            jax.ShapeDtypeStruct((slots, width + quarter), BF),
        ],
        compiler_params=pltpu.CompilerParams(vmem_limit_bytes=24 * 1024 * 1024),
        name="norm_pack",
    )(place, *sums, residual, gain, main_hot, extra_hot)


def regroup_matrix(transposed):
    size = 32 * QUARTERS * EXTRA
    grouped = lax.broadcasted_iota(jnp.int32, (size, size), 1 if transposed else 0)
    plain = lax.broadcasted_iota(jnp.int32, (size, size), 0 if transposed else 1)
    c, rest = grouped // (32 * EXTRA), grouped % (32 * EXTRA)
    source = (rest // EXTRA) * (QUARTERS * EXTRA) + c * EXTRA + rest % EXTRA
    return (source == plain).astype(F32).astype(BF)


def regroup(extra, parts):
    size = 32 * QUARTERS * EXTRA
    per = 32 * EXTRA
    swap = regroup_matrix(False)
    for g in range(extra.shape[0] // size):
        rows = dot(swap, extra[g * size : (g + 1) * size, :]).astype(BF)
        for c in range(QUARTERS):
            parts[c, g * per : (g + 1) * per, :] = rows[c * per : (c + 1) * per, :]


def ungroup(parts, out):
    size = 32 * QUARTERS * EXTRA
    per = 32 * EXTRA
    swap = regroup_matrix(True)
    for g in range(out.shape[0] // size):
        rows = jnp.concatenate([parts[c, g * per : (g + 1) * per, :] for c in range(QUARTERS)], axis=0)
        out[g * size : (g + 1) * size, :] = dot(swap, rows).astype(BF)


def up_step(step, rows, weights, acc, act):
    hidden = act.shape[1]

    @pl.when(step == 0)
    def _():
        @pl.loop(0, acc.shape[0] // 64)
        def _(r):
            acc[pl.ds(pl.multiple_of(r * 64, 64), 64), :] = jnp.zeros((64, acc.shape[1]), F32)

    acc[...] += dot(rows, weights)

    @pl.when(step == QUARTERS - 1)
    def _():
        gate = acc[:, :hidden]
        act[...] = (gate / (1.0 + jnp.exp(-gate)) * acc[:, hidden:]).astype(BF)


def main_kernel(after, main, w_in, w_down, out, acc, act):
    step = pl.program_id(0)

    @pl.when(step < QUARTERS)
    def _():
        up_step(step, main[...], w_in[...], acc, act)

    @pl.when(step >= QUARTERS)
    def _():
        out[...] = dot(act[...], w_down[...]).astype(BF)


def extra_kernel(extra, w_in, w_down, out, acc, act, parts):
    step = pl.program_id(0)

    @pl.when(step == 0)
    def _():
        regroup(extra, parts)

    @pl.when(step < QUARTERS)
    def _():
        rows = w_in.shape[0] // QUARTERS
        up_step(step, parts[step], w_in[pl.ds(pl.multiple_of(step * rows, rows), rows), :], acc, act)

    @pl.when(step >= QUARTERS)
    def _():
        columns = w_down.shape[1] // QUARTERS
        lanes = pl.ds(pl.multiple_of((step - QUARTERS) * columns, columns), columns)
        parts[step - QUARTERS] = dot(act[...], w_down[:, lanes]).astype(BF)

    @pl.when(step == 2 * QUARTERS - 1)
    def _():
        ungroup(parts, out)


def run_expert(incoming, w_in, w_down, after=None):
    slots = incoming.shape[0]
    width = w_in.shape[0]
    hidden = w_down.shape[0]
    quarter = width // QUARTERS
    last = QUARTERS - 1
    main = after is not None
    rows = slots if main else slots // MAIN * EXTRA
    if main:
        in_specs = [
            pl.BlockSpec(memory_space=pl.ANY),
            pl.BlockSpec((slots, quarter), lambda i: (0, jnp.minimum(i, last))),
        ]
        out_specs = pl.BlockSpec((slots, quarter), lambda i: (0, jnp.maximum(i - QUARTERS, 0)))
        out_width, scratch = width, []
    else:
        in_specs = [pl.BlockSpec((slots, quarter), lambda i: (0, QUARTERS))]
        out_specs = pl.BlockSpec((slots, quarter), lambda i: (0, 0))
        out_width, scratch = quarter, [pltpu.VMEM((QUARTERS, rows, quarter), BF)]
    return pl.pallas_call(
        main_kernel if main else extra_kernel,
        grid=(2 * QUARTERS,),
        in_specs=in_specs
        + (
            [
                pl.BlockSpec((quarter, 2 * hidden), lambda i: (jnp.minimum(i, last), 0)),
                pl.BlockSpec((hidden, quarter), lambda i: (0, jnp.clip(i - QUARTERS, 0, last))),
            ]
            if main
            else [pl.BlockSpec(memory_space=pltpu.VMEM)] * 2
        ),
        out_specs=out_specs,
        out_shape=jax.ShapeDtypeStruct((slots, out_width), BF),
        scratch_shapes=[pltpu.VMEM((rows, 2 * hidden), F32), pltpu.VMEM((rows, hidden), BF)] + scratch,
        compiler_params=pltpu.CompilerParams(vmem_limit_bytes=VMEM_LIMIT if main else 20 * 1024 * 1024),
        name="experts_main" if main else "experts_extra",
    )(*([after] if main else []), incoming, w_in, w_down)


def select_dots(dots, keys):
    slot = lax.broadcasted_iota(jnp.int32, dots.shape, 1)
    column = lax.broadcasted_iota(jnp.int32, (dots.shape[0], 128), 1)
    picked = jnp.zeros((dots.shape[0], 128), F32)
    for k in range(keys.shape[1]):
        entry = jnp.sum(jnp.where(slot == keys[:, k : k + 1], dots[...], 0.0), axis=1, keepdims=True)
        picked = jnp.where(column == k, entry, picked)
    return picked


def combine_step(rows, hidden, cot, gates, out, dots):
    step = pl.program_id(0)
    tokens = hidden.shape[0]
    mixed = dot(gates[...], rows)
    out[...] = (hidden[...] + (mixed[:tokens] + mixed[tokens:])).astype(out.dtype)
    more = lax.dot_general(cot[...], rows, (((1,), (1,)), ((), ())), preferred_element_type=F32)

    @pl.when(step == 0)
    def _():
        dots[...] = more

    @pl.when(step > 0)
    def _():
        dots[...] += more


def combine_extra(extra, hidden, cot, gates, keys, out, grad, dots, parts):
    step = pl.program_id(0)

    @pl.when(step == 0)
    def _():
        regroup(extra, parts)

    combine_step(parts[step], hidden, cot, gates, out, dots)

    @pl.when(step == QUARTERS - 1)
    def _():
        grad[...] = select_dots(dots, keys)


def combine_main(main, hidden, cot, gates, keys, before, out, grad, dots):
    combine_step(main[...], hidden, cot, gates, out, dots)

    @pl.when(pl.program_id(0) == QUARTERS - 1)
    def _():
        grad[...] = (select_dots(dots, keys) + before[...]).T[: keys.shape[1], :]


def combine(returned, hidden, cot, gates, keys, before=None):
    slots = returned.shape[0]
    tokens, width = hidden.shape
    quarter = width // QUARTERS
    top = keys.shape[1]
    count = gates.shape[1]
    whole = lambda shape: pl.BlockSpec(shape, lambda i: (0, 0))
    part = lambda shape: pl.BlockSpec(shape, lambda i: (0, i))
    main = before is not None
    more = [before] if main else []
    grad = (top, tokens) if main else (tokens, 128)
    return pl.pallas_call(
        combine_main if main else combine_extra,
        grid=(QUARTERS,),
        in_specs=[
            part((slots, quarter)) if main else whole((slots, quarter)),
            part((tokens, quarter)),
            part((tokens, quarter)),
        ]
        + [whole(a.shape) for a in (gates, keys, *more)],
        out_specs=[part((tokens, quarter)), whole(grad)],
        out_shape=[
            jax.ShapeDtypeStruct((tokens, width), BF if main else F32),
            jax.ShapeDtypeStruct(grad, F32),
        ],
        scratch_shapes=[pltpu.VMEM((tokens, count), F32)]
        + ([] if main else [pltpu.VMEM((QUARTERS, count, quarter), BF)]),
        compiler_params=pltpu.CompilerParams(vmem_limit_bytes=VMEM_LIMIT if main else 20 * 1024 * 1024),
        name="combine_main" if main else "combine_extra",
    )(returned, hidden, cot, gates, keys, *more)


def split_in_two(values):
    high = values.astype(BF)
    return jnp.concatenate([high, (values - high.astype(F32)).astype(BF)], axis=0)


def routing(chosen, gates, experts):
    tokens = chosen.shape[0]
    hits = chosen[:, :, None] == jnp.arange(experts, dtype=jnp.int32)[None, None, :]
    member = jnp.any(hits, axis=1)
    earlier = jnp.arange(tokens)[None, :] < jnp.arange(tokens)[:, None]
    rank = dot(earlier.astype(BF), member.astype(BF)).astype(jnp.int32)
    rank = jnp.where(member, rank, -1)
    gate_of = jnp.sum(jnp.where(hits, gates[:, :, None], 0.0), axis=1)
    pair_rank = jnp.sum(jnp.where(hits, rank[:, None, :], 0), axis=2)

    is_main = rank[:, :, None] == jnp.arange(MAIN, dtype=jnp.int32)
    extra_row = jnp.arange(QUARTERS * EXTRA, dtype=jnp.int32)
    is_extra = rank[:, :, None] == MAIN + extra_row % EXTRA
    main_hot = is_main.astype(BF).transpose(1, 2, 0).reshape(experts * MAIN, tokens)
    in_quarter = extra_row[None, :, None, None] // EXTRA == jnp.arange(QUARTERS)[None, None, :, None]
    extra_hot = (is_extra.transpose(1, 2, 0)[:, :, None, :] & in_quarter).astype(BF)
    extra_hot = extra_hot.reshape(experts * QUARTERS * EXTRA, QUARTERS * tokens)

    gates_main = jnp.where(is_main, gate_of[:, :, None], 0.0).reshape(tokens, experts * MAIN)
    is_extra = rank[:, :, None] == MAIN + jnp.arange(EXTRA, dtype=jnp.int32)
    gates_extra = jnp.where(is_extra, gate_of[:, :, None], 0.0).reshape(tokens, experts * EXTRA)
    keys_main = jnp.where(pair_rank < MAIN, chosen * MAIN + pair_rank, -1)
    keys_extra = jnp.where(pair_rank >= MAIN, chosen * EXTRA + pair_rank - MAIN, -1)
    return main_hot, extra_hot, split_in_two(gates_main), split_in_two(gates_extra), keys_main, keys_extra


def layer(
    queries,
    rotated_keys,
    projected_values,
    doc_ids,
    residual,
    out_weight,
    norm_gain,
    routes,
    gate_vals,
    cotangent,
    expert_in,
    expert_down,
):
    seq_count = lax.axis_size("seq")
    experts = seq_count * lax.axis_size("exp")
    tokens, width = residual.shape[1:]
    along_x, along_z = lambda d: exp_shift(0, d), lambda d: exp_shift(d, 0)
    half = out_weight.shape[0] // 2
    upper = gather_line(out_weight[:half], along_x)
    lower = gather_line(out_weight[half:], along_z)

    by_head = lambda a: a[0].reshape(tokens, seq_count, -1)
    heads = jnp.concatenate([by_head(queries), by_head(rotated_keys), by_head(projected_values)], axis=2)
    heads = lax.all_to_all(heads.transpose(1, 0, 2), "seq", split_axis=0, concat_axis=0, tiled=True)
    heads, upper, lower = lax.optimization_barrier((heads, upper, lower))
    upper, lower = gather_plane(upper, along_z), gather_plane(lower, along_x)
    heads = heads.reshape(seq_count * tokens, -1)
    q_width = width // seq_count
    attended = attend_heads(
        heads[:, :q_width],
        heads[:, q_width : q_width + HEAD_SIZE],
        heads[:, q_width + HEAD_SIZE :],
        doc_ids[0],
    )
    other = lax.ppermute(attended, "exp", exp_shift(0, 0, 1))
    seq, exp = lax.axis_index("seq"), lax.axis_index("exp")
    place = jnp.stack([seq, exp // (RING * CORES), exp // CORES % RING, exp % CORES]).astype(jnp.int32)
    sums = list(project(place, attended, other, upper, lower, seq_count))
    for index in range(1, len(sums)):
        core, shift = divmod(index, seq_count)
        around = [
            (s * RING * RING * CORES + a, (s + shift) % seq_count * RING * RING * CORES + b)
            for s in range(seq_count)
            for a, b in exp_shift(0, 0, core)
        ]
        sums[index] = lax.ppermute(sums[index], ("seq", "exp"), around)

    main_hot, extra_hot, gates_main, gates_extra, keys_main, keys_extra = routing(routes[0], gate_vals[0], experts)
    hidden, outgoing = pack(place, sums, residual[0], norm_gain[None, :], main_hot, extra_hot)

    def exchange(slots):
        blocks = slots.reshape(experts, MAIN, slots.shape[1])
        blocks = lax.all_to_all(blocks, ("seq", "exp"), split_axis=0, concat_axis=0, tiled=True)
        return blocks.reshape(slots.shape)

    incoming = exchange(outgoing)
    results = run_expert(incoming, expert_in[0], expert_down[0])
    returned = exchange(results)
    main_results = run_expert(incoming, expert_in[0], expert_down[0], after=results)
    cot = cotangent[0]
    hidden, grad = combine(returned, hidden, cot, gates_extra, keys_extra)
    returned = exchange(main_results)
    layer_out, gate_grad = combine(returned, hidden, cot, gates_main, keys_main, grad)
    return layer_out[None], gate_grad.T[None]


def solution(mesh):
    in_specs = (
        P("exp", "seq", None),
        P("exp", "seq", None),
        P("exp", "seq", None),
        P("exp", None),
        P("exp", "seq", None),
        P("seq", "exp"),
        P(),
        P("exp", "seq", None),
        P("exp", "seq", None),
        P("exp", "seq", None),
        P(("seq", "exp"), None, None),
        P(("seq", "exp"), None, None),
    )
    out_specs = (P("exp", "seq", None), P("exp", "seq", None))
    return jax.shard_map(layer, mesh=mesh, in_specs=in_specs, out_specs=out_specs, check_vma=False)
```

```python
import math

import jax
import jax.numpy as jnp
from jax import lax
from jax.experimental import pallas as pl
from jax.experimental.pallas import tpu as pltpu
from jax.sharding import PartitionSpec as P

QUERY_HEADS = 32
KEY_VALUE_HEADS = 4
HEAD_SIZE = 128
MAIN = 8
EXTRA = 2
QUARTERS = 4
BF = jnp.bfloat16
F32 = jnp.float32
VMEM_LIMIT = 60 * 1024 * 1024
RING = 4
CORES = 2


def dot(a, b):
    return jnp.dot(a, b, preferred_element_type=F32)


def attend_heads(q_heads, k_heads, v_heads, doc_rows):
    length = q_heads.shape[0]
    group = QUERY_HEADS // KEY_VALUE_HEADS
    score_scale = 1.0 / math.sqrt(HEAD_SIZE)
    positions = jnp.arange(length)
    allowed = (positions[None, :] <= positions[:, None]) & (doc_rows[None, :] == doc_rows[:, None])
    query_block = q_heads.reshape(length, group, HEAD_SIZE)
    scores = jnp.einsum("rgd,jd->grj", query_block, k_heads, preferred_element_type=F32) * score_scale
    scores = jnp.where(allowed[None], scores, -jnp.inf)
    row_max = jnp.max(scores, axis=-1, keepdims=True)
    raised = jnp.exp(scores - row_max)
    weights_bf = (raised / jnp.sum(raised, axis=-1, keepdims=True)).astype(BF)
    block_out = jnp.einsum("grj,jd->rgd", weights_bf, v_heads, preferred_element_type=F32)
    return block_out.astype(BF).reshape(length, group * HEAD_SIZE)


def exp_shift(along_z, along_x, other_core=0):
    def place(z, x, core):
        return (z % RING * RING + x % RING) * CORES + core % CORES

    return [
        (place(z, x, core), place(z + along_z, x + along_x, core + other_core))
        for z in range(RING)
        for x in range(RING)
        for core in range(CORES)
    ]


def gather_line(part, shifts):
    return jnp.stack(gather_plane(part, shifts))


def gather_plane(line, shifts):
    gathered = [line]
    for d in range(1, RING):
        gathered.append(lax.ppermute(line, "exp", shifts(d)))
    return gathered


def project_kernel(place, mine, other, *rest):
    pieces, outs = rest[: 2 * RING], rest[2 * RING : -3]
    weight, result, arrived = rest[-3:]
    step = pl.program_id(0)
    tokens, block = outs[0].shape
    length = mine.shape[0]
    half = weight.shape[0] // 2

    @pl.when(step == 0)
    def _():
        copies = []
        for k in range(RING):
            for m in range(RING):
                for lower in range(2):
                    z, x = (m, k) if lower else (k, m)
                    chip = lax.rem(place[1] + RING - z, RING) * RING + lax.rem(place[2] + RING - x, RING)
                    lanes = pl.ds(pl.multiple_of(chip * 128, 128), 128)
                    copies.append(
                        pltpu.make_async_copy(
                            pieces[lower * RING + k].at[m],
                            weight.at[pl.ds(lower * half, half), lanes],
                            arrived.at[(k * RING + m) * 2 + lower],
                        )
                    )
        for copy in copies:
            copy.start()
        for copy in copies:
            copy.wait()

    columns = weight[:, pl.ds(pl.multiple_of(step * block, block), block)]
    result[:length, :] = dot(mine[...], columns)
    result[length:, :] = dot(other[...], columns)
    for index, out in enumerate(outs):
        pack_of, shift = divmod(index, length // tokens)
        start = pack_of * length + lax.rem(place[0] + shift, length // tokens) * tokens
        out[...] = result[pl.ds(pl.multiple_of(start, tokens), tokens), :].astype(out.dtype)


def project(place, mine, other, upper, lower, seq_count):
    length, inner = mine.shape
    tokens = length // seq_count
    width = RING * RING * 128
    steps = 4
    block = width // steps
    count = CORES * seq_count
    return pl.pallas_call(
        project_kernel,
        grid_spec=pltpu.PrefetchScalarGridSpec(
            num_scalar_prefetch=1,
            grid=(steps,),
            in_specs=[pl.BlockSpec((length, inner), lambda i, _: (0, 0))] * 2
            + [pl.BlockSpec(memory_space=pl.ANY)] * (2 * RING),
            out_specs=[pl.BlockSpec((tokens, block), lambda i, _: (0, i))] * count,
            scratch_shapes=[
                pltpu.VMEM((inner, width), BF),
                pltpu.VMEM((CORES * length, block), F32),
                pltpu.SemaphoreType.DMA((2 * RING * RING,)),
            ],
        ),
        out_shape=[jax.ShapeDtypeStruct((tokens, width), F32 if k == 0 else BF) for k in range(count)],
        compiler_params=pltpu.CompilerParams(vmem_limit_bytes=VMEM_LIMIT),
        name="project",
    )(place, mine, other, *upper, *lower)


def pack_kernel(place, *refs):
    *sums, residual, gain, main_hot, extra_hot, hidden, out, stacked = refs
    step = pl.program_id(0)
    tokens = residual.shape[0]
    quarter = stacked.shape[1]
    per_core = len(sums) // CORES

    @pl.when(step == 0)
    def _():
        total = jnp.zeros((tokens, 128), F32)
        for core in range(CORES):
            parts = sums[core * per_core : (core + 1) * per_core]
            for chip in range(RING * RING):
                value = parts[0][:, chip * 128 : (chip + 1) * 128].astype(F32)
                for part in parts[1:]:
                    value += part[:, chip * 128 : (chip + 1) * 128].astype(F32)
                shard = chip * CORES + lax.rem(place[3] + core, CORES)
                lanes = pl.ds(pl.multiple_of(shard * 128, 128), 128)
                state = residual[:, lanes].astype(F32) + value
                hidden[:, lanes] = state
                total += state * state
        mean = jnp.sum(total, axis=-1, keepdims=True) * (1.0 / hidden.shape[1])
        scale = 1.0 / jnp.sqrt(mean + 1e-06)
        for c in range(QUARTERS):
            lanes = slice(c * quarter, (c + 1) * quarter)
            stacked[c * tokens : (c + 1) * tokens, :] = (hidden[:, lanes] * scale * gain[:, lanes]).astype(BF)

    @pl.when(step < QUARTERS)
    def _():
        rows = stacked[pl.ds(pl.multiple_of(step * tokens, tokens), tokens), :]
        out[...] = dot(main_hot[...], rows).astype(BF)

    @pl.when(step == QUARTERS)
    def _():
        out[...] = dot(extra_hot[...], stacked[...]).astype(BF)


def pack(place, sums, residual, gain, main_hot, extra_hot):
    tokens, width = residual.shape
    quarter = width // QUARTERS
    slots = main_hot.shape[0]
    whole = lambda shape: pl.BlockSpec(shape, lambda i, _: (0, 0))
    return pl.pallas_call(
        pack_kernel,
        grid_spec=pltpu.PrefetchScalarGridSpec(
            num_scalar_prefetch=1,
            grid=(QUARTERS + 1,),
            in_specs=[whole(a.shape) for a in (*sums, residual, gain, main_hot, extra_hot)],
            out_specs=[whole((tokens, width)), pl.BlockSpec((slots, quarter), lambda i, _: (0, i))],
            scratch_shapes=[pltpu.VMEM((QUARTERS * tokens, quarter), BF)],
        ),
        out_shape=[
            jax.ShapeDtypeStruct((tokens, width), F32),
            jax.ShapeDtypeStruct((slots, width + quarter), BF),
        ],
        compiler_params=pltpu.CompilerParams(vmem_limit_bytes=24 * 1024 * 1024),
        name="norm_pack",
    )(place, *sums, residual, gain, main_hot, extra_hot)


def regroup_matrix(transposed):
    size = 32 * QUARTERS * EXTRA
    grouped = lax.broadcasted_iota(jnp.int32, (size, size), 1 if transposed else 0)
    plain = lax.broadcasted_iota(jnp.int32, (size, size), 0 if transposed else 1)
    c, rest = grouped // (32 * EXTRA), grouped % (32 * EXTRA)
    source = (rest // EXTRA) * (QUARTERS * EXTRA) + c * EXTRA + rest % EXTRA
    return (source == plain).astype(F32).astype(BF)


def regroup(extra, parts):
    size = 32 * QUARTERS * EXTRA
    per = 32 * EXTRA
    swap = regroup_matrix(False)
    for g in range(extra.shape[0] // size):
        rows = dot(swap, extra[g * size : (g + 1) * size, :]).astype(BF)
        for c in range(QUARTERS):
            parts[c, g * per : (g + 1) * per, :] = rows[c * per : (c + 1) * per, :]


def ungroup(parts, out):
    size = 32 * QUARTERS * EXTRA
    per = 32 * EXTRA
    swap = regroup_matrix(True)
    for g in range(out.shape[0] // size):
        rows = jnp.concatenate([parts[c, g * per : (g + 1) * per, :] for c in range(QUARTERS)], axis=0)
        out[g * size : (g + 1) * size, :] = dot(swap, rows).astype(BF)


def up_step(step, rows, weights, acc, act):
    hidden = act.shape[1]

    @pl.when(step == 0)
    def _():
        @pl.loop(0, acc.shape[0] // 64)
        def _(r):
            acc[pl.ds(pl.multiple_of(r * 64, 64), 64), :] = jnp.zeros((64, acc.shape[1]), F32)

    acc[...] += dot(rows, weights)

    @pl.when(step == QUARTERS - 1)
    def _():
        gate = acc[:, :hidden]
        act[...] = (gate / (1.0 + jnp.exp(-gate)) * acc[:, hidden:]).astype(BF)


def main_kernel(after, main, w_in, w_down, out, acc, act):
    step = pl.program_id(0)

    @pl.when(step < QUARTERS)
    def _():
        up_step(step, main[...], w_in[...], acc, act)

    @pl.when(step >= QUARTERS)
    def _():
        out[...] = dot(act[...], w_down[...]).astype(BF)


def extra_kernel(extra, w_in, w_down, out, acc, act, parts):
    step = pl.program_id(0)

    @pl.when(step == 0)
    def _():
        regroup(extra, parts)

    @pl.when(step < QUARTERS)
    def _():
        rows = w_in.shape[0] // QUARTERS
        up_step(step, parts[step], w_in[pl.ds(pl.multiple_of(step * rows, rows), rows), :], acc, act)

    @pl.when(step >= QUARTERS)
    def _():
        columns = w_down.shape[1] // QUARTERS
        lanes = pl.ds(pl.multiple_of((step - QUARTERS) * columns, columns), columns)
        parts[step - QUARTERS] = dot(act[...], w_down[:, lanes]).astype(BF)

    @pl.when(step == 2 * QUARTERS - 1)
    def _():
        ungroup(parts, out)


def run_expert(incoming, w_in, w_down, after=None):
    slots = incoming.shape[0]
    width = w_in.shape[0]
    hidden = w_down.shape[0]
    quarter = width // QUARTERS
    last = QUARTERS - 1
    main = after is not None
    rows = slots if main else slots // MAIN * EXTRA
    if main:
        in_specs = [
            pl.BlockSpec(memory_space=pl.ANY),
            pl.BlockSpec((slots, quarter), lambda i: (0, jnp.minimum(i, last))),
        ]
        out_specs = pl.BlockSpec((slots, quarter), lambda i: (0, jnp.maximum(i - QUARTERS, 0)))
        out_width, scratch = width, []
    else:
        in_specs = [pl.BlockSpec((slots, quarter), lambda i: (0, QUARTERS))]
        out_specs = pl.BlockSpec((slots, quarter), lambda i: (0, 0))
        out_width, scratch = quarter, [pltpu.VMEM((QUARTERS, rows, quarter), BF)]
    return pl.pallas_call(
        main_kernel if main else extra_kernel,
        grid=(2 * QUARTERS,),
        in_specs=in_specs
        + (
            [
                pl.BlockSpec((quarter, 2 * hidden), lambda i: (jnp.minimum(i, last), 0)),
                pl.BlockSpec((hidden, quarter), lambda i: (0, jnp.clip(i - QUARTERS, 0, last))),
            ]
            if main
            else [pl.BlockSpec(memory_space=pltpu.VMEM)] * 2
        ),
        out_specs=out_specs,
        out_shape=jax.ShapeDtypeStruct((slots, out_width), BF),
        scratch_shapes=[pltpu.VMEM((rows, 2 * hidden), F32), pltpu.VMEM((rows, hidden), BF)] + scratch,
        compiler_params=pltpu.CompilerParams(vmem_limit_bytes=VMEM_LIMIT if main else 20 * 1024 * 1024),
        name="experts_main" if main else "experts_extra",
    )(*([after] if main else []), incoming, w_in, w_down)


def select_dots(dots, keys):
    slot = lax.broadcasted_iota(jnp.int32, dots.shape, 1)
    column = lax.broadcasted_iota(jnp.int32, (dots.shape[0], 128), 1)
    picked = jnp.zeros((dots.shape[0], 128), F32)
    for k in range(keys.shape[1]):
        entry = jnp.sum(jnp.where(slot == keys[:, k : k + 1], dots[...], 0.0), axis=1, keepdims=True)
        picked = jnp.where(column == k, entry, picked)
    return picked


def combine_step(rows, hidden, cot, gates, out, dots):
    step = pl.program_id(0)
    tokens = hidden.shape[0]
    mixed = dot(gates[...], rows)
    out[...] = (hidden[...] + (mixed[:tokens] + mixed[tokens:])).astype(out.dtype)
    more = lax.dot_general(cot[...], rows, (((1,), (1,)), ((), ())), preferred_element_type=F32)

    @pl.when(step == 0)
    def _():
        dots[...] = more

    @pl.when(step > 0)
    def _():
        dots[...] += more


def combine_extra(extra, hidden, cot, gates, keys, out, grad, dots, parts):
    step = pl.program_id(0)

    @pl.when(step == 0)
    def _():
        regroup(extra, parts)

    combine_step(parts[step], hidden, cot, gates, out, dots)

    @pl.when(step == QUARTERS - 1)
    def _():
        grad[...] = select_dots(dots, keys)


def combine_main(main, hidden, cot, gates, keys, before, out, grad, dots):
    combine_step(main[...], hidden, cot, gates, out, dots)

    @pl.when(pl.program_id(0) == QUARTERS - 1)
    def _():
        grad[...] = (select_dots(dots, keys) + before[...]).T[: keys.shape[1], :]


def combine(returned, hidden, cot, gates, keys, before=None):
    slots = returned.shape[0]
    tokens, width = hidden.shape
    quarter = width // QUARTERS
    top = keys.shape[1]
    count = gates.shape[1]
    whole = lambda shape: pl.BlockSpec(shape, lambda i: (0, 0))
    part = lambda shape: pl.BlockSpec(shape, lambda i: (0, i))
    main = before is not None
    more = [before] if main else []
    grad = (top, tokens) if main else (tokens, 128)
    return pl.pallas_call(
        combine_main if main else combine_extra,
        grid=(QUARTERS,),
        in_specs=[
            part((slots, quarter)) if main else whole((slots, quarter)),
            part((tokens, quarter)),
            part((tokens, quarter)),
        ]
        + [whole(a.shape) for a in (gates, keys, *more)],
        out_specs=[part((tokens, quarter)), whole(grad)],
        out_shape=[
            jax.ShapeDtypeStruct((tokens, width), BF if main else F32),
            jax.ShapeDtypeStruct(grad, F32),
        ],
        scratch_shapes=[pltpu.VMEM((tokens, count), F32)]
        + ([] if main else [pltpu.VMEM((QUARTERS, count, quarter), BF)]),
        compiler_params=pltpu.CompilerParams(vmem_limit_bytes=VMEM_LIMIT if main else 20 * 1024 * 1024),
        name="combine_main" if main else "combine_extra",
    )(returned, hidden, cot, gates, keys, *more)


def split_in_two(values):
    high = values.astype(BF)
    return jnp.concatenate([high, (values - high.astype(F32)).astype(BF)], axis=0)


def routing(chosen, gates, experts):
    tokens = chosen.shape[0]
    hits = chosen[:, :, None] == jnp.arange(experts, dtype=jnp.int32)[None, None, :]
    member = jnp.any(hits, axis=1)
    earlier = jnp.arange(tokens)[None, :] < jnp.arange(tokens)[:, None]
    rank = dot(earlier.astype(BF), member.astype(BF)).astype(jnp.int32)
    rank = jnp.where(member, rank, -1)
    gate_of = jnp.sum(jnp.where(hits, gates[:, :, None], 0.0), axis=1)
    pair_rank = jnp.sum(jnp.where(hits, rank[:, None, :], 0), axis=2)

    is_main = rank[:, :, None] == jnp.arange(MAIN, dtype=jnp.int32)
    extra_row = jnp.arange(QUARTERS * EXTRA, dtype=jnp.int32)
    is_extra = rank[:, :, None] == MAIN + extra_row % EXTRA
    main_hot = is_main.astype(BF).transpose(1, 2, 0).reshape(experts * MAIN, tokens)
    in_quarter = extra_row[None, :, None, None] // EXTRA == jnp.arange(QUARTERS)[None, None, :, None]
    extra_hot = (is_extra.transpose(1, 2, 0)[:, :, None, :] & in_quarter).astype(BF)
    extra_hot = extra_hot.reshape(experts * QUARTERS * EXTRA, QUARTERS * tokens)

    gates_main = jnp.where(is_main, gate_of[:, :, None], 0.0).reshape(tokens, experts * MAIN)
    is_extra = rank[:, :, None] == MAIN + jnp.arange(EXTRA, dtype=jnp.int32)
    gates_extra = jnp.where(is_extra, gate_of[:, :, None], 0.0).reshape(tokens, experts * EXTRA)
    keys_main = jnp.where(pair_rank < MAIN, chosen * MAIN + pair_rank, -1)
    keys_extra = jnp.where(pair_rank >= MAIN, chosen * EXTRA + pair_rank - MAIN, -1)
    return main_hot, extra_hot, split_in_two(gates_main), split_in_two(gates_extra), keys_main, keys_extra


def layer(
    queries,
    rotated_keys,
    projected_values,
    doc_ids,
    residual,
    out_weight,
    norm_gain,
    routes,
    gate_vals,
    cotangent,
    expert_in,
    expert_down,
):
    seq_count = lax.axis_size("seq")
    experts = seq_count * lax.axis_size("exp")
    tokens, width = residual.shape[1:]
    along_x, along_z = lambda d: exp_shift(0, d), lambda d: exp_shift(d, 0)
    half = out_weight.shape[0] // 2
    upper = gather_line(out_weight[:half], along_x)
    lower = gather_line(out_weight[half:], along_z)

    by_head = lambda a: a[0].reshape(tokens, seq_count, -1)
    heads = jnp.concatenate([by_head(queries), by_head(rotated_keys), by_head(projected_values)], axis=2)
    heads = heads.transpose(1, 0, 2)
    heads = lax.all_to_all(heads, "seq", split_axis=0, concat_axis=0, tiled=True)
    upper, lower = gather_plane(upper, along_z), gather_plane(lower, along_x)
    heads = heads.reshape(seq_count * tokens, -1)
    q_width = width // seq_count
    attended = attend_heads(
        heads[:, :q_width],
        heads[:, q_width : q_width + HEAD_SIZE],
        heads[:, q_width + HEAD_SIZE :],
        doc_ids[0],
    )
    other = lax.ppermute(attended, "exp", exp_shift(0, 0, 1))
    seq, exp = lax.axis_index("seq"), lax.axis_index("exp")
    place = jnp.stack([seq, exp // (RING * CORES), exp // CORES % RING, exp % CORES]).astype(jnp.int32)
    sums = list(project(place, attended, other, upper, lower, seq_count))
    for index in range(1, len(sums)):
        core, shift = divmod(index, seq_count)
        around = [
            (s * RING * RING * CORES + a, (s + shift) % seq_count * RING * RING * CORES + b)
            for s in range(seq_count)
            for a, b in exp_shift(0, 0, core)
        ]
        sums[index] = lax.ppermute(sums[index], ("seq", "exp"), around)

    main_hot, extra_hot, gates_main, gates_extra, keys_main, keys_extra = routing(routes[0], gate_vals[0], experts)
    hidden, outgoing = pack(place, sums, residual[0], norm_gain[None, :], main_hot, extra_hot)

    def exchange(slots):
        blocks = slots.reshape(experts, MAIN, slots.shape[1])
        blocks = lax.all_to_all(blocks, ("seq", "exp"), split_axis=0, concat_axis=0, tiled=True)
        return blocks.reshape(slots.shape)

    incoming = exchange(outgoing)
    results = run_expert(incoming, expert_in[0], expert_down[0])
    returned = exchange(results)
    main_results = run_expert(incoming, expert_in[0], expert_down[0], after=results)
    cot = cotangent[0]
    hidden, grad = combine(returned, hidden, cot, gates_extra, keys_extra)
    returned = exchange(main_results)
    layer_out, gate_grad = combine(returned, hidden, cot, gates_main, keys_main, grad)
    return layer_out[None], gate_grad.T[None]


def solution(mesh):
    in_specs = (
        P("exp", "seq", None),
        P("exp", "seq", None),
        P("exp", "seq", None),
        P("exp", None),
        P("exp", "seq", None),
        P("seq", "exp"),
        P(),
        P("exp", "seq", None),
        P("exp", "seq", None),
        P("exp", "seq", None),
        P(("seq", "exp"), None, None),
        P(("seq", "exp"), None, None),
    )
    out_specs = (P("exp", "seq", None), P("exp", "seq", None))
    return jax.shard_map(layer, mesh=mesh, in_specs=in_specs, out_specs=out_specs, check_vma=False)
```
